32 devices in a mesh: grp: 2 (over x), wide: 16 (over z, y, core).
Axes of the slice: x: 2, y: 2, z: 4, core: 2. Of those that a mesh axis runs over, the one named last changes fastest.
Arguments:
- raw: bfloat16 [4096, 16, 2048], P(('grp', 'wide')), parts along dimension 0, may hold values from -6 to 6
- cell_feed: int32 [1024], replicated, may hold values from 0 to 1023, each once
- dm_delay: int32 [1024, 1024], replicated, may hold values from 0 to 15
Outputs:
- dedispersed: float32 [2048, 16, 1024], P(('grp', 'wide')), parts along dimension 0
The draws below stay inside these ranges and needn't reach their ends.
There are 2 independent parts, one for each index of `grp`. The reference program is written for one: setup_inputs(seed, part) draws one part's arguments, and reference() takes and returns one part's arrays. A program takes and returns all parts, laid end to end along the dimension named above; an argument that names none is the same for every part. Nothing has to cross between parts.
Inputs may be any that keep to these rules, and one draw needn't show every extreme that they name: `cell_feed`: every antenna stands at exactly one cell.
All inputs are finite; a program needn't handle non-finite values.
Results may differ from the reference program's by a relative error of at most 0.0084.
Values may be sent and summed in bfloat16 or wider, within the bound.
No kernel may reach another device: no remote copies, remote signals or barrier semaphores. Data moves between devices by JAX's collectives and lax.ppermute only.
A program may use at most 128 MiB of HBM per device.

```python
import math
import jax
import jax.numpy as jnp
import numpy as np
from jax import lax

NFEED = 2048
NFREQ = 1024
SAMP = 2048
BEAMS = 1024
DMS = 1024
FRAMES = 16


def with_ends(entries, key, least, high):
    extent = entries.shape
    place = [jax.random.randint(jax.random.fold_in(key, axis), (), 0, extent[axis]) for axis in range(len(extent))]
    entries = entries.at[tuple(place)].set(least)
    longest = extent.index(max(extent))
    place[longest] = (place[longest] + 1) % extent[longest]
    return entries.at[tuple(place)].set(high)


def level_of(stream_key, shape, shards, low, largest):
    loudness = 1.0
    for dim, parts in shards:
        draws = jax.random.uniform(jax.random.fold_in(jax.random.fold_in(stream_key, 6), dim), (parts,), jnp.float32, low / len(shards), largest / len(shards))
        loudness = loudness * jnp.repeat(jnp.exp(draws), shape[dim] // parts).reshape((-1,) + (1,) * (len(shape) - 1 - dim))
    return loudness


def scatter_about(key, shape, spread, reach, split=(), kind=jnp.bfloat16):
    values = spread * jax.random.normal(key, shape, jnp.float32)
    if split:
        values = values * level_of(key, shape, split, -0.22, 0.18)
    return jnp.clip(values, -reach, reach).astype(kind)


def setup_inputs(seed: int = 0, part: int = 0) -> dict:
    key_of = jax.random.split(jax.random.key(seed), 4)
    part_splits = jax.random.split(jax.random.fold_in(key_of[3], part), 4)
    raw = scatter_about(part_splits[0], (NFEED, FRAMES, SAMP), 1.0, 6.0, ((0, 16),))
    cell_feed = jax.random.permutation(key_of[1], BEAMS).astype(jnp.int32)
    dm_delay = with_ends(jax.random.randint(key_of[2], (DMS, NFREQ), 0, FRAMES), jax.random.fold_in(key_of[2], 1), 0, FRAMES - 1).astype(jnp.int32)
    return {"raw": raw, "cell_feed": cell_feed, "dm_delay": dm_delay}


EAST_COSINE = np.array([[1, 1, 1, 1], [1, 0, -1, 0], [1, -1, 1, -1], [1, 0, -1, 0]], np.float32)
EAST_SINE = np.array([[0, 0, 0, 0], [0, 1, 0, -1], [0, 0, 0, 0], [0, -1, 0, 1]], np.float32)

def phase_pair(count, length):
    angle = (count % length).astype(jnp.float32) * (2.0 * math.pi / length)
    return (jnp.cos(angle), jnp.sin(angle))

def channel_table(samples, first, width):
    sample_ids = lax.broadcasted_iota(jnp.int32, (samples, width), 0)
    freq_ids = lax.broadcasted_iota(jnp.int32, (samples, width), 1) + first
    cosine, sine = phase_pair(sample_ids * freq_ids, samples)
    factor = 1.0 / math.sqrt(samples)
    return jnp.concatenate([cosine * factor, -sine * factor], axis=1).astype(jnp.bfloat16)

def sky_table(cells):
    rows = lax.broadcasted_iota(jnp.int32, (cells, cells), 0)
    cols = lax.broadcasted_iota(jnp.int32, (cells, cells), 1)
    cosine, sine = phase_pair(rows * cols, cells)
    real_row = jnp.stack([cosine, sine], axis=-1)
    imag_row = jnp.stack([-sine, cosine], axis=-1)
    factor = 1.0 / math.sqrt(cells)
    return (jnp.stack([real_row, imag_row], axis=1) * factor).astype(jnp.bfloat16)

def transform_table(frames):
    terms = frames // 2 + 1
    harmonic = lax.broadcasted_iota(jnp.int32, (terms, frames), 0)
    moment = lax.broadcasted_iota(jnp.int32, (terms, frames), 1)
    cosine, sine = phase_pair(harmonic * moment, frames)
    return jnp.stack([cosine, -sine]).astype(jnp.bfloat16)

def beam_power(spec, feed_index, table):
    grid = jnp.take(spec, feed_index.reshape(-1), axis=0)
    grid = grid.reshape(feed_index.shape + spec.shape[1:])
    beams = jnp.einsum('joni,penrif->poerfj', table.astype(jnp.float32), grid.astype(jnp.float32), precision=lax.Precision.HIGHEST)
    real_part = beams[:, 0]
    imag_part = beams[:, 1]
    cosines = jnp.asarray(EAST_COSINE)
    sines = jnp.asarray(EAST_SINE)
    high = lax.Precision.HIGHEST
    east_real = 0.5 * (jnp.einsum('qe,perfj->prfqj', cosines, real_part, precision=high) + jnp.einsum('qe,perfj->prfqj', sines, imag_part, precision=high))
    east_imag = 0.5 * (jnp.einsum('qe,perfj->prfqj', cosines, imag_part, precision=high) - jnp.einsum('qe,perfj->prfqj', sines, real_part, precision=high))
    power = 0.5 * lax.optimization_barrier(jnp.sum(east_real * east_real + east_imag * east_imag, axis=0))
    return power.reshape(power.shape[0], power.shape[1], -1)

def reference(raw, cell_feed, dm_delay):
    nfeed, frames, samples = raw.shape
    nfreq = samples // 2
    fblock = math.gcd(nfreq, 64)
    cells = cell_feed.shape[0] // 4
    polar = lax.broadcasted_iota(jnp.int32, (2, 4, cells), 0)
    feed_index = 2 * cell_feed.reshape(1, 4, cells).astype(jnp.int32) + polar
    table_sky = sky_table(cells)
    flat = raw.reshape(nfeed * frames, samples).astype(jnp.float32)

    def one_block(index):
        table = channel_table(samples, index * fblock, fblock).astype(jnp.float32)
        spectra = jnp.dot(flat, table, precision=lax.Precision.HIGHEST).astype(jnp.bfloat16)
        return beam_power(spectra.reshape(nfeed, frames, 2, fblock), feed_index, table_sky)
    power = lax.map(one_block, jnp.arange(nfreq // fblock, dtype=jnp.int32))
    power = jnp.moveaxis(power, 0, 1).reshape(frames, nfreq, -1)
    intensity = (power - lax.optimization_barrier(jnp.mean(power, axis=0, keepdims=True))).astype(jnp.bfloat16)
    spectrum = jnp.einsum('okr,rfb->kofb', transform_table(frames).astype(jnp.float32), intensity.astype(jnp.float32), precision=lax.Precision.HIGHEST).astype(jnp.bfloat16)

    def one_term(term):
        harmonic, block = term
        cosine, sine = phase_pair(harmonic * dm_delay, frames)
        factors = jnp.stack([cosine, sine]).astype(jnp.bfloat16).astype(jnp.float32)
        products = jnp.einsum('ofb,udf->boud', block.astype(jnp.float32), factors, precision=lax.Precision.HIGHEST)
        real_part = products[:, 0, 0] - products[:, 1, 1]
        imag_part = products[:, 0, 1] + products[:, 1, 0]
        return jnp.stack([real_part, imag_part], axis=1)
    terms = frames // 2 + 1
    trials = lax.map(one_term, (jnp.arange(terms, dtype=jnp.int32), spectrum))
    moment = lax.broadcasted_iota(jnp.int32, (frames, terms), 0)
    harmonic = lax.broadcasted_iota(jnp.int32, (frames, terms), 1)
    cosine, sine = phase_pair(moment * harmonic, frames)
    weight = jnp.where((harmonic == 0) | (harmonic * 2 == frames), 1.0, 2.0).astype(jnp.float32)
    weight = weight / (frames * math.sqrt(nfreq))
    table = jnp.stack([cosine * weight, -sine * weight], axis=1)
    return jnp.einsum('tuk,kbud->btd', table, trials, precision=lax.Precision.HIGHEST)
```

```python
import functools
import math

import jax
import jax.numpy as jnp
import numpy as np
from jax import lax
from jax.experimental import pallas as pl
from jax.experimental.pallas import tpu as pltpu
from jax.sharding import PartitionSpec as P

LANES = 128
FIRST_SHARE = 0.5
VMEM_LIMIT = 60000 * 1024

EAST_COSINE = np.array([[1, 1, 1, 1], [1, 0, -1, 0], [1, -1, 1, -1], [1, 0, -1, 0]], np.float32)
EAST_SINE = np.array([[0, 0, 0, 0], [0, 1, 0, -1], [0, 0, 0, 0], [0, -1, 0, 1]], np.float32)


def phase_pair(count, length):
    angle = (count % length).astype(jnp.float32) * (2.0 * math.pi / length)
    return (jnp.cos(angle), jnp.sin(angle))


def channel_table(samples, width):
    sample_ids = lax.broadcasted_iota(jnp.int32, (samples, width), 0)
    freq_ids = lax.broadcasted_iota(jnp.int32, (samples, width), 1)
    cosine, sine = phase_pair(sample_ids * freq_ids, samples)
    factor = 1.0 / math.sqrt(samples)
    return jnp.concatenate([cosine * factor, -sine * factor], axis=1).astype(jnp.bfloat16)


def sky_table(cells):
    rows = lax.broadcasted_iota(jnp.int32, (cells, cells), 0)
    cols = lax.broadcasted_iota(jnp.int32, (cells, cells), 1)
    cosine, sine = phase_pair(rows * cols, cells)
    real_row = jnp.stack([cosine, sine], axis=-1)
    imag_row = jnp.stack([-sine, cosine], axis=-1)
    factor = 1.0 / math.sqrt(cells)
    return (jnp.stack([real_row, imag_row], axis=1) * factor).astype(jnp.bfloat16)


def transform_table(frames):
    terms = frames // 2 + 1
    harmonic = lax.broadcasted_iota(jnp.int32, (terms, frames), 0)
    moment = lax.broadcasted_iota(jnp.int32, (terms, frames), 1)
    cosine, sine = phase_pair(harmonic * moment, frames)
    return jnp.stack([cosine, -sine]).astype(jnp.bfloat16)


def beam_power(spec, feed_index, table):
    grid = jnp.take(spec, feed_index.reshape(-1), axis=0)
    grid = grid.reshape(feed_index.shape + spec.shape[1:])
    beams = jnp.einsum("joni,penrif->poerfj", table, grid, preferred_element_type=jnp.float32)
    real_part = beams[:, 0]
    imag_part = beams[:, 1]
    cosines = jnp.asarray(EAST_COSINE)
    sines = jnp.asarray(EAST_SINE)
    high = lax.Precision.HIGHEST
    east_real = 0.5 * (
        jnp.einsum("qe,perfj->prfqj", cosines, real_part, precision=high)
        + jnp.einsum("qe,perfj->prfqj", sines, imag_part, precision=high)
    )
    east_imag = 0.5 * (
        jnp.einsum("qe,perfj->prfqj", cosines, imag_part, precision=high)
        - jnp.einsum("qe,perfj->prfqj", sines, real_part, precision=high)
    )
    power = 0.5 * jnp.sum(east_real * east_real + east_imag * east_imag, axis=0)
    return power.reshape(power.shape[0], power.shape[1], -1)


def dedisperse(spectrum, dm_delay, frames):
    base_cos, base_sin = phase_pair(jnp.transpose(dm_delay), frames)
    beams_dev = spectrum.shape[3]
    nfreq = spectrum.shape[2]

    def one_term(carry, block):
        cosine, sine = carry
        cos_half = cosine.astype(jnp.bfloat16)
        sin_half = sine.astype(jnp.bfloat16)
        upper = jnp.concatenate([cos_half, sin_half], axis=1)
        lower = jnp.concatenate([-sin_half, cos_half], axis=1)
        right = jnp.concatenate([upper, lower], axis=0)
        left = block.reshape(2 * nfreq, beams_dev)
        result = lax.dot_general(
            left, right, (((0,), (0,)), ((), ())), preferred_element_type=jnp.float32
        )
        next_cos = cosine * base_cos - sine * base_sin
        next_sin = sine * base_cos + cosine * base_sin
        return ((next_cos, next_sin), result)

    start = (jnp.ones(base_cos.shape, jnp.float32), jnp.zeros(base_cos.shape, jnp.float32))
    final, trials = lax.scan(one_term, start, spectrum)
    return trials.reshape(trials.shape[0], beams_dev, 2, -1)


def synthesis(trials, frames, nfreq):
    terms = frames // 2 + 1
    moment = lax.broadcasted_iota(jnp.int32, (frames, terms), 0)
    harmonic = lax.broadcasted_iota(jnp.int32, (frames, terms), 1)
    cosine, sine = phase_pair(moment * harmonic, frames)
    weight = jnp.where((harmonic == 0) | (harmonic * 2 == frames), 1.0, 2.0).astype(jnp.float32)
    weight = weight / (frames * math.sqrt(nfreq))
    table = jnp.stack([cosine * weight, -sine * weight], axis=1)
    return jnp.einsum("tuk,kbud->btd", table, trials, precision=lax.Precision.HIGHEST)


def plain_body(raw, cell_feed, dm_delay):
    feed_dev, frames, samples = raw.shape
    nfreq = samples // 2
    table = channel_table(samples, nfreq)
    spectra = jnp.dot(
        raw.reshape(feed_dev * frames, samples), table, preferred_element_type=jnp.float32
    )
    spectra = spectra.astype(jnp.bfloat16).reshape(feed_dev, frames, 2, nfreq)
    cells = cell_feed.shape[0] // 4
    polar = lax.broadcasted_iota(jnp.int32, (2, 4, cells), 0)
    feed_index = 2 * cell_feed.reshape(1, 4, cells) + polar
    table_sky = sky_table(cells)
    arrived = lax.all_to_all(spectra, "wide", split_axis=3, concat_axis=0, tiled=True)
    power = beam_power(arrived, feed_index, table_sky)
    centred = (power - jnp.mean(power, axis=0, keepdims=True)).astype(jnp.bfloat16)
    time_table = transform_table(frames)
    local = jnp.einsum("okr,rfb->kofb", time_table, centred, preferred_element_type=jnp.float32)
    spectrum = lax.all_to_all(
        local.astype(jnp.bfloat16), "wide", split_axis=3, concat_axis=2, tiled=True
    )
    trials = dedisperse(spectrum, dm_delay, frames)
    return synthesis(trials, frames, nfreq)


def params(steps=1):
    return pltpu.CompilerParams(
        dimension_semantics=("arbitrary",) * steps, vmem_limit_bytes=VMEM_LIMIT
    )


def cost(flops, nbytes):
    return pl.CostEstimate(flops=int(flops), bytes_accessed=int(nbytes), transcendentals=0)


def angle_tables(samples, parts, kdev, low):
    freq = (np.arange(parts)[:, None, None] * kdev + np.arange(kdev)).repeat(2, axis=1).reshape(-1)
    quarter = np.tile(np.repeat(np.arange(2), kdev), parts) * (samples // 4)
    coarse = np.arange(0, samples, low)[:, None] * freq[None, :] % samples
    fine = (np.arange(low)[:, None] * freq[None, :] + quarter[None, :]) % samples
    turn = 2.0 * np.pi / samples
    factor = 1.0 / math.sqrt(samples)
    first = np.stack([np.cos(coarse * turn), np.sin(coarse * turn)]).astype(np.float32)
    second = np.stack([np.cos(fine * turn), np.sin(fine * turn)]) * factor
    return first, second.astype(np.float32)


def row_order(antennas, frames, first, count):
    r, p, a = np.meshgrid(
        np.arange(first, first + count), np.arange(2), np.arange(antennas), indexing="ij"
    )
    source = ((a * 2 + p) * frames + r).reshape(-1)
    return (source[:, None] == np.arange(antennas * 2 * frames)[None, :]).astype(np.float32)


def channelise_kernel(low, wide_cols, coarse_ref, fine_ref, order_ref, raw_ref, out_ref, table, rows):
    samples = table.shape[1]
    count = out_ref.shape[1]
    group = out_ref.shape[3]

    @pl.when(pl.program_id(0) == 0)
    def _():
        def make(block, carry):
            at = pl.multiple_of(block * low, low)
            for part in range(table.shape[0]):
                cols = slice(part * wide_cols, (part + 1) * wide_cols)
                cos_a = coarse_ref[0, pl.ds(block, 1), cols]
                sin_a = coarse_ref[1, pl.ds(block, 1), cols]
                value = cos_a * fine_ref[0, :, cols] - sin_a * fine_ref[1, :, cols]
                table[part, pl.ds(at, low), :] = value.astype(jnp.bfloat16)
            return carry

        lax.fori_loop(0, samples // low, make, 0)

    source = raw_ref[...].reshape(-1, samples)
    rows[...] = jnp.dot(order_ref[...], source, preferred_element_type=jnp.float32).astype(
        jnp.bfloat16
    )

    def one(part, carry):
        value = jnp.dot(rows[...], table[part], preferred_element_type=jnp.float32)
        value = value.astype(jnp.bfloat16)
        per = wide_cols // LANES
        for piece in range(per):
            block = value[:, piece * LANES : (piece + 1) * LANES]
            out_ref[part * per + piece] = block.reshape(count, 2, group, LANES)
        return carry

    lax.fori_loop(0, table.shape[0], one, 0)


def channelise(raw, first, count, parts):
    feed_dev, frames, samples = raw.shape
    cols = samples
    kdev = samples // 2 // parts
    low = 64
    wide_cols = 2 * LANES
    group = 16
    steps = feed_dev // (2 * group)
    coarse, fine = angle_tables(samples, parts, kdev, low)
    order = row_order(group, frames, first, count)
    kernel = functools.partial(channelise_kernel, low, wide_cols)
    whole = lambda shape: pl.BlockSpec(shape, lambda i: (0,) * len(shape))
    return pl.pallas_call(
        kernel,
        name="channelise",
        grid=(steps,),
        in_specs=[
            whole(coarse.shape),
            whole(fine.shape),
            whole(order.shape),
            pl.BlockSpec((2 * group, frames, samples), lambda i: (i, 0, 0)),
        ],
        out_specs=pl.BlockSpec((parts, count, 2, group, LANES), lambda i: (0, 0, 0, i, 0)),
        out_shape=jax.ShapeDtypeStruct((parts, count, 2, feed_dev // 2, LANES), jnp.bfloat16),
        scratch_shapes=[
            pltpu.VMEM((cols // wide_cols, samples, wide_cols), jnp.bfloat16),
            pltpu.VMEM((order.shape[0], samples), jnp.bfloat16),
        ],
        compiler_params=params(),
        cost_estimate=cost(
            2 * feed_dev * count * samples * (cols + order.shape[1]), 2 * raw.size + 2 * raw.size
        ),
    )(jnp.asarray(coarse), jnp.asarray(fine), jnp.asarray(order, jnp.bfloat16), raw)


def beam_table(cell_feed):
    beams = cell_feed.shape[0]
    cells = beams // 4
    antenna = lax.broadcasted_iota(jnp.int32, (beams, beams), 0)
    cell = lax.broadcasted_iota(jnp.int32, (beams, beams), 1)
    place = jnp.sum(jnp.where(cell_feed[None, :] == antenna, cell, 0), axis=1)
    shape = (2, beams, beams)
    part = lax.broadcasted_iota(jnp.int32, shape, 0)
    beam = lax.broadcasted_iota(jnp.int32, shape, 1)
    east = (place // cells)[None, None, :]
    north = (place % cells)[None, None, :]
    quarter = cells // 4
    count = quarter * ((beam // cells) * east) + (beam % cells) * north + quarter * part
    angle = (count % cells).astype(jnp.float32) * (2.0 * math.pi / cells)
    return (jnp.cos(angle) * (1.0 / math.sqrt(cells))).astype(jnp.bfloat16)


def beam_kernel(tile, weight_ref, spec_ref, out_ref, right):
    srcs, pair, pols, group, lanes = spec_ref.shape
    beams = weight_ref.shape[1]
    half = lanes // 2
    for r in range(pair):
        for p in range(pols):
            at = (r * pols + p) * lanes
            right[:, at : at + lanes] = spec_ref[:, r, p].reshape(srcs * group, lanes)
    lane = lax.broadcasted_iota(jnp.int32, (tile, lanes), 1)
    low = lane < half
    sign = jnp.where(low, -1.0, 1.0)

    def one(step, carry):
        at = pl.multiple_of(step * tile, tile)
        first = jnp.dot(
            weight_ref[0, pl.ds(at, tile), :], right[...], preferred_element_type=jnp.float32
        )
        second = jnp.dot(
            weight_ref[1, pl.ds(at, tile), :], right[...], preferred_element_type=jnp.float32
        )
        sums = []
        for r in range(pair):
            total = None
            for p in range(pols):
                cut = slice((r * pols + p) * lanes, (r * pols + p + 1) * lanes)
                turned = pltpu.roll(second[:, cut], half, 1)
                value = first[:, cut] + sign * turned
                total = value * value if total is None else total + value * value
            sums.append(0.125 * (total + pltpu.roll(total, half, 1)))
        out_ref[0, pl.ds(at, tile), :] = jnp.where(low, sums[0], sums[1])
        return carry

    lax.fori_loop(0, beams // tile, one, 0)


def beam_stage(weights, arrived):
    srcs, count, pols, group, lanes = arrived.shape
    beams = weights.shape[1]
    return pl.pallas_call(
        functools.partial(beam_kernel, 256),
        name="beams",
        grid=(count // 2,),
        in_specs=[
            pl.BlockSpec(weights.shape, lambda i: (0, 0, 0)),
            pl.BlockSpec((srcs, 2, pols, group, lanes), lambda i: (0, i, 0, 0, 0)),
        ],
        out_specs=pl.BlockSpec((1, beams, lanes), lambda i: (i, 0, 0)),
        out_shape=jax.ShapeDtypeStruct((count // 2, beams, lanes), jnp.float32),
        scratch_shapes=[pltpu.VMEM((srcs * group, 2 * pols * lanes), jnp.bfloat16)],
        compiler_params=params(),
        cost_estimate=cost(4 * beams * beams * count * pols * lanes, 2 * arrived.size),
    )(weights, arrived)


def centre_kernel(frames, *refs):
    out_ref = refs[-1]
    blocks = [ref[i] for ref in refs[:-1] for i in range(ref.shape[0])]
    total = functools.reduce(lambda a, b: a + b, blocks)
    lanes = total.shape[-1]
    mean = (total + pltpu.roll(total, lanes // 2, 1)) * (1.0 / frames)
    for i, block in enumerate(blocks):
        out_ref[0, i] = (block - mean).astype(jnp.bfloat16)


def centre(powers, frames, parts):
    beams, lanes = powers[0].shape[1:]
    own = beams // parts
    return pl.pallas_call(
        functools.partial(centre_kernel, frames),
        name="centre",
        grid=(parts,),
        in_specs=[
            pl.BlockSpec((power.shape[0], own, lanes), lambda i: (0, i, 0)) for power in powers
        ],
        out_specs=pl.BlockSpec((1, frames // 2, own, lanes), lambda i: (i, 0, 0, 0)),
        out_shape=jax.ShapeDtypeStruct((parts, frames // 2, own, lanes), jnp.bfloat16),
        compiler_params=params(),
        cost_estimate=cost(frames * beams * lanes, 6 * frames * beams * lanes // 2),
    )(*powers)


def turn_value(count, frames):
    folded = jnp.minimum(count, frames - count)
    inner = jnp.minimum(folded, frames // 2 - folded)
    value = jnp.zeros(count.shape, jnp.float32)
    for i in range(frames // 4):
        value = jnp.where(inner == i, np.float32(math.cos(2.0 * math.pi * i / frames)), value)
    return jnp.where(folded > frames // 4, -value, value)


def factor_kernel(frames, delay_ref, out_ref):
    delay = delay_ref[...]
    half = frames // 2
    for h in range(1, half):
        count = (h * delay) & (frames - 1)
        shifted = (count + (frames - frames // 4)) & (frames - 1)
        out_ref[2 * h - 2] = turn_value(count, frames).astype(jnp.bfloat16)
        out_ref[2 * h - 1] = turn_value(shifted, frames).astype(jnp.bfloat16)
    out_ref[2 * half - 2] = jnp.where((delay & 1) == 1, -1.0, 1.0).astype(jnp.bfloat16)


def factor_stage(delay, frames):
    nfreq, trials = delay.shape
    rows = 32
    terms = frames - 1
    return pl.pallas_call(
        functools.partial(factor_kernel, frames),
        name="factors",
        grid=(nfreq // rows,),
        in_specs=[pl.BlockSpec((rows, trials), lambda i: (i, 0))],
        out_specs=pl.BlockSpec((terms, rows, trials), lambda i: (0, i, 0)),
        out_shape=jax.ShapeDtypeStruct((terms, nfreq, trials), jnp.bfloat16),
        compiler_params=params(),
        cost_estimate=cost(10 * terms * nfreq * trials, 2 * terms * nfreq * trials),
    )(delay)


def rounded(value):
    return float(np.asarray(value, np.float32).astype(jnp.bfloat16).astype(np.float32))


def turns(count, frames):
    angle = 2.0 * math.pi * (count % frames) / frames
    pair = []
    for value in (math.cos(angle), math.sin(angle)):
        pair.append(float(round(value)) if abs(value - round(value)) < 1e-12 else value)
    return pair


def weighted(terms):
    total = None
    for factor, value in terms:
        if factor == 0.0:
            continue
        term = value if factor == 1.0 else (-value if factor == -1.0 else factor * value)
        total = term if total is None else total + term
    return total


def harmonics_of(values, frames):
    half, quarter = frames // 2, frames // 4
    plus = [values[r] + values[r + half] for r in range(half)]
    minus = [values[r] - values[r + half] for r in range(half)]
    result = []
    for h in range(half + 1):
        base = minus if h % 2 else plus
        real, imag = [(1.0, base[0])], []
        for r in range(1, quarter):
            cosine, sine = (rounded(x) for x in turns(h * r, frames))
            other = base[half - r]
            even = base[r] - other if h % 2 else base[r] + other
            odd = base[r] + other if h % 2 else base[r] - other
            real.append((cosine, even))
            imag.append((-sine, odd))
        cosine, sine = (rounded(x) for x in turns(h * quarter, frames))
        real.append((cosine, base[quarter]))
        imag.append((-sine, base[quarter]))
        result.append((weighted(real), weighted(imag)))
    return result


def dedisperse_kernel(frames, nfreq, arrived_ref, factor_ref, out_ref, left, zero):
    srcs, pairs, own, lanes = arrived_ref.shape
    half = frames // 2
    tile = factor_ref.shape[2]

    @pl.when(pl.program_id(0) == 0)
    def _():
        low = lax.broadcasted_iota(jnp.int32, (own, lanes), 1) < lanes // 2
        zero[...] = jnp.zeros_like(zero)

        def one(j, carry):
            values = []
            for i in range(pairs):
                even = arrived_ref[2 * j, i].astype(jnp.float32)
                odd = arrived_ref[2 * j + 1, i].astype(jnp.float32)
                values.append(jnp.where(low, even, pltpu.roll(odd, lanes // 2, 1)))
                values.append(jnp.where(low, pltpu.roll(even, lanes // 2, 1), odd))
            parts = harmonics_of(values, frames)
            zero[...] += parts[0][0].astype(jnp.bfloat16).astype(jnp.float32)
            for h in range(1, half + 1):
                left[j, h - 1, :own, :] = parts[h][0].astype(jnp.bfloat16)
                if h < half:
                    left[j, h - 1, own:, :] = parts[h][1].astype(jnp.bfloat16)
            return carry

        lax.fori_loop(0, srcs // 2, one, 0)

    scale = 1.0 / (frames * math.sqrt(nfreq))
    first = scale * jnp.sum(zero[...], axis=1, keepdims=True)
    real, imag = [], []
    for h in range(1, half):
        block = jnp.concatenate([left[j, h - 1] for j in range(srcs // 2)], axis=1)
        by_cos = jnp.dot(block, factor_ref[2 * h - 2], preferred_element_type=jnp.float32)
        by_sin = jnp.dot(block, factor_ref[2 * h - 1], preferred_element_type=jnp.float32)
        real.append((2.0 * scale) * (by_cos[:own] - by_sin[own:]))
        imag.append((2.0 * scale) * (by_sin[:own] + by_cos[own:]))
    block = jnp.concatenate([left[j, half - 1, :own, :] for j in range(srcs // 2)], axis=1)
    last = scale * jnp.dot(block, factor_ref[2 * half - 2], preferred_element_type=jnp.float32)
    for t in range(half):
        parts = []
        for parity in range(2):
            terms = []
            for h in range(2 - parity, half, 2):
                cosine, sine = turns(h * t, frames)
                terms.append((cosine, real[h - 1]))
                terms.append((-sine, imag[h - 1]))
            parts.append(weighted(terms))
        even = parts[0] + first + (last if t % 2 == 0 else -last)
        out_ref[:, t, :] = even + parts[1]
        out_ref[:, t + half, :] = even - parts[1]


def dedisperse_stage(arrived, factors, frames):
    srcs, pairs, own, lanes = arrived.shape
    terms, nfreq, trials = factors.shape
    tile = 2 * LANES
    return pl.pallas_call(
        functools.partial(dedisperse_kernel, frames, nfreq),
        name="dedisperse",
        grid=(trials // tile,),
        in_specs=[
            pl.BlockSpec(arrived.shape, lambda i: (0, 0, 0, 0)),
            pl.BlockSpec((terms, nfreq, tile), lambda i: (0, 0, i)),
        ],
        out_specs=pl.BlockSpec((own, frames, tile), lambda i: (0, 0, i)),
        out_shape=jax.ShapeDtypeStruct((own, frames, trials), jnp.float32),
        scratch_shapes=[
            pltpu.VMEM((srcs // 2, frames // 2, 2 * own, lanes), jnp.bfloat16),
            pltpu.VMEM((own, lanes), jnp.float32),
        ],
        compiler_params=params(),
        cost_estimate=cost(4 * own * terms * nfreq * trials, 2 * factors.size + 4 * own * frames * trials),
    )(arrived, factors)


def tiled_body(parts, raw, cell_feed, dm_delay):
    feed_dev, frames, samples = raw.shape
    head = 2 * max(1, int(frames // 2 * FIRST_SHARE))
    cuts = [(0, head), (head, frames - head)]
    message = channelise(raw, cuts[0][0], cuts[0][1], parts)
    raw, cell_feed, dm_delay, message = lax.optimization_barrier(
        (raw, cell_feed, dm_delay, message)
    )
    messages = [message] + [channelise(raw, first, count, parts) for first, count in cuts[1:]]
    weights = beam_table(cell_feed)
    factors = factor_stage(jnp.transpose(dm_delay), frames)
    powers = []
    for message in messages:
        arrived = lax.all_to_all(message, "wide", split_axis=0, concat_axis=0, tiled=True)
        powers.append(beam_stage(weights, arrived))
    centred = centre(powers, frames, parts)
    arrived = lax.all_to_all(centred, "wide", split_axis=0, concat_axis=0, tiled=True)
    return dedisperse_stage(arrived, factors, frames)


def fits(parts, raw_shape, cells, delay_shape):
    feed_dev, frames, samples = raw_shape
    trials, nfreq = delay_shape
    return (
        samples // parts == LANES
        and nfreq * 2 == samples
        and samples % (2 * LANES) == 0
        and feed_dev % 32 == 0
        and frames % 16 == 0
        and frames & (frames - 1) == 0
        and cells % (256) == 0
        and cells // parts == LANES // 2
        and trials % (2 * LANES) == 0
        and parts % 2 == 0
    )


def solution(mesh):
    parts = mesh.shape["wide"]

    def body(raw, cell_feed, dm_delay):
        if fits(parts, raw.shape, cell_feed.shape[0], dm_delay.shape):
            return tiled_body(parts, raw, cell_feed, dm_delay)
        return plain_body(raw, cell_feed, dm_delay)

    placed = (P(("grp", "wide"), None, None), P(), P())
    return jax.shard_map(
        body, mesh=mesh, in_specs=placed, out_specs=P(("grp", "wide"), None, None), check_vma=False
    )
```

```python
import functools
import math

import jax
import jax.numpy as jnp
import numpy as np
from jax import lax
from jax.experimental import pallas as pl
from jax.experimental.pallas import tpu as pltpu
from jax.sharding import PartitionSpec as P

LANES = 128
VMEM_LIMIT = 60000 * 1024

EAST_COSINE = np.array([[1, 1, 1, 1], [1, 0, -1, 0], [1, -1, 1, -1], [1, 0, -1, 0]], np.float32)
EAST_SINE = np.array([[0, 0, 0, 0], [0, 1, 0, -1], [0, 0, 0, 0], [0, -1, 0, 1]], np.float32)


def phase_pair(count, length):
    angle = (count % length).astype(jnp.float32) * (2.0 * math.pi / length)
    return (jnp.cos(angle), jnp.sin(angle))


def channel_table(samples, width):
    sample_ids = lax.broadcasted_iota(jnp.int32, (samples, width), 0)
    freq_ids = lax.broadcasted_iota(jnp.int32, (samples, width), 1)
    cosine, sine = phase_pair(sample_ids * freq_ids, samples)
    factor = 1.0 / math.sqrt(samples)
    return jnp.concatenate([cosine * factor, -sine * factor], axis=1).astype(jnp.bfloat16)


def sky_table(cells):
    rows = lax.broadcasted_iota(jnp.int32, (cells, cells), 0)
    cols = lax.broadcasted_iota(jnp.int32, (cells, cells), 1)
    cosine, sine = phase_pair(rows * cols, cells)
    real_row = jnp.stack([cosine, sine], axis=-1)
    imag_row = jnp.stack([-sine, cosine], axis=-1)
    factor = 1.0 / math.sqrt(cells)
    return (jnp.stack([real_row, imag_row], axis=1) * factor).astype(jnp.bfloat16)


def transform_table(frames):
    terms = frames // 2 + 1
    harmonic = lax.broadcasted_iota(jnp.int32, (terms, frames), 0)
    moment = lax.broadcasted_iota(jnp.int32, (terms, frames), 1)
    cosine, sine = phase_pair(harmonic * moment, frames)
    return jnp.stack([cosine, -sine]).astype(jnp.bfloat16)


def beam_power(spec, feed_index, table):
    grid = jnp.take(spec, feed_index.reshape(-1), axis=0)
    grid = grid.reshape(feed_index.shape + spec.shape[1:])
    beams = jnp.einsum("joni,penrif->poerfj", table, grid, preferred_element_type=jnp.float32)
    real_part = beams[:, 0]
    imag_part = beams[:, 1]
    cosines = jnp.asarray(EAST_COSINE)
    sines = jnp.asarray(EAST_SINE)
    high = lax.Precision.HIGHEST
    east_real = 0.5 * (
        jnp.einsum("qe,perfj->prfqj", cosines, real_part, precision=high)
        + jnp.einsum("qe,perfj->prfqj", sines, imag_part, precision=high)
    )
    east_imag = 0.5 * (
        jnp.einsum("qe,perfj->prfqj", cosines, imag_part, precision=high)
        - jnp.einsum("qe,perfj->prfqj", sines, real_part, precision=high)
    )
    power = 0.5 * jnp.sum(east_real * east_real + east_imag * east_imag, axis=0)
    return power.reshape(power.shape[0], power.shape[1], -1)


def dedisperse(spectrum, dm_delay, frames):
    base_cos, base_sin = phase_pair(jnp.transpose(dm_delay), frames)
    beams_dev = spectrum.shape[3]
    nfreq = spectrum.shape[2]

    def one_term(carry, block):
        cosine, sine = carry
        cos_half = cosine.astype(jnp.bfloat16)
        sin_half = sine.astype(jnp.bfloat16)
        upper = jnp.concatenate([cos_half, sin_half], axis=1)
        lower = jnp.concatenate([-sin_half, cos_half], axis=1)
        right = jnp.concatenate([upper, lower], axis=0)
        left = block.reshape(2 * nfreq, beams_dev)
        result = lax.dot_general(
            left, right, (((0,), (0,)), ((), ())), preferred_element_type=jnp.float32
        )
        next_cos = cosine * base_cos - sine * base_sin
        next_sin = sine * base_cos + cosine * base_sin
        return ((next_cos, next_sin), result)

    start = (jnp.ones(base_cos.shape, jnp.float32), jnp.zeros(base_cos.shape, jnp.float32))
    final, trials = lax.scan(one_term, start, spectrum)
    return trials.reshape(trials.shape[0], beams_dev, 2, -1)


def synthesis(trials, frames, nfreq):
    terms = frames // 2 + 1
    moment = lax.broadcasted_iota(jnp.int32, (frames, terms), 0)
    harmonic = lax.broadcasted_iota(jnp.int32, (frames, terms), 1)
    cosine, sine = phase_pair(moment * harmonic, frames)
    weight = jnp.where((harmonic == 0) | (harmonic * 2 == frames), 1.0, 2.0).astype(jnp.float32)
    weight = weight / (frames * math.sqrt(nfreq))
    table = jnp.stack([cosine * weight, -sine * weight], axis=1)
    return jnp.einsum("tuk,kbud->btd", table, trials, precision=lax.Precision.HIGHEST)


def plain_body(raw, cell_feed, dm_delay):
    feed_dev, frames, samples = raw.shape
    nfreq = samples // 2
    table = channel_table(samples, nfreq)
    spectra = jnp.dot(
        raw.reshape(feed_dev * frames, samples), table, preferred_element_type=jnp.float32
    )
    spectra = spectra.astype(jnp.bfloat16).reshape(feed_dev, frames, 2, nfreq)
    cells = cell_feed.shape[0] // 4
    polar = lax.broadcasted_iota(jnp.int32, (2, 4, cells), 0)
    feed_index = 2 * cell_feed.reshape(1, 4, cells) + polar
    table_sky = sky_table(cells)
    arrived = lax.all_to_all(spectra, "wide", split_axis=3, concat_axis=0, tiled=True)
    power = beam_power(arrived, feed_index, table_sky)
    centred = (power - jnp.mean(power, axis=0, keepdims=True)).astype(jnp.bfloat16)
    time_table = transform_table(frames)
    local = jnp.einsum("okr,rfb->kofb", time_table, centred, preferred_element_type=jnp.float32)
    spectrum = lax.all_to_all(
        local.astype(jnp.bfloat16), "wide", split_axis=3, concat_axis=2, tiled=True
    )
    trials = dedisperse(spectrum, dm_delay, frames)
    return synthesis(trials, frames, nfreq)


def params(steps=1):
    return pltpu.CompilerParams(
        dimension_semantics=("arbitrary",) * steps, vmem_limit_bytes=VMEM_LIMIT
    )


def cost(flops, nbytes):
    return pl.CostEstimate(flops=int(flops), bytes_accessed=int(nbytes), transcendentals=0)


def angle_tables(samples, parts, kdev, low):
    freq = np.arange(parts)[:, None] * kdev + np.tile(np.arange(kdev), 2)[None, :]
    quarter = np.repeat(np.arange(2), kdev) * (samples // 4)
    coarse = np.arange(0, samples, low)[None, :, None] * freq[:, None, :] % samples
    fine = (np.arange(low)[None, :, None] * freq[:, None, :] + quarter) % samples
    turn = 2.0 * np.pi / samples
    factor = 1.0 / math.sqrt(samples)
    first = np.stack([np.cos(coarse * turn), np.sin(coarse * turn)])
    second = np.stack([np.cos(fine * turn), np.sin(fine * turn)]) * factor
    return first.astype(np.float32), second.astype(np.float32)


def row_order(antennas, frames, first, count):
    r, p, a = np.meshgrid(
        np.arange(first, first + count), np.arange(2), np.arange(antennas), indexing="ij"
    )
    source = ((a * 2 + p) * frames + r).reshape(-1)
    return (source[:, None] == np.arange(antennas * 2 * frames)[None, :]).astype(np.float32)


def channelise_kernel(low, me_ref, coarse_ref, fine_ref, order_ref, raw_ref, *refs):
    split = len(refs) > 3
    out_refs, table, rows = (refs[:-3], *refs[-3:-1]) if split else (refs[:1], *refs[1:])
    out_ref = refs[-1] if split else refs[0]
    pairs, samples, wide_cols = table.shape
    parts, count, pols, antennas, lanes = out_ref.shape
    own = order_ref.shape[0]
    steps = rows.shape[0] // own
    group = antennas // steps
    step = pl.program_id(0)

    @pl.when(step == 0)
    def _():
        def make(pair, carry):
            for side in range(2):
                part = lax.rem(me_ref[0] + 2 * pair + side, parts)
                fine_cos, fine_sin = fine_ref[0, part], fine_ref[1, part]
                for block in range(samples // low):
                    cos_a = coarse_ref[0, part, block : block + 1, :]
                    sin_a = coarse_ref[1, part, block : block + 1, :]
                    value = cos_a * fine_cos - sin_a * fine_sin
                    table[
                        pair, block * low : (block + 1) * low, side * lanes : (side + 1) * lanes
                    ] = value.astype(jnp.bfloat16)
            return carry

        lax.fori_loop(0, pairs, make, 0)

    source = raw_ref[...].reshape(-1, samples)
    ordered = jnp.dot(order_ref[...], source, preferred_element_type=jnp.float32)
    rows[pl.ds(pl.multiple_of(step * own, own), own), :] = ordered.astype(jnp.bfloat16)

    @pl.when(step == steps - 1)
    def _():
        def one(pair, carry):
            value = jnp.dot(rows[...], table[pair], preferred_element_type=jnp.float32)
            value = value.astype(jnp.bfloat16)
            for side in range(2):
                for i in range(steps):
                    block = value[i * own : (i + 1) * own, side * lanes : (side + 1) * lanes]
                    out_ref[2 * pair + side, :, :, i * group : (i + 1) * group, :] = block.reshape(
                        count, pols, group, lanes
                    )
            return carry

        lax.fori_loop(0, pairs, one, 0)
        if split:
            for part in range(parts):
                out_refs[part][...] = out_ref[part]


def channelise(raw, me, first, count, parts, split):
    feed_dev, frames, samples = raw.shape
    kdev = samples // 2 // parts
    low = 64
    group = 16
    steps = feed_dev // (2 * group)
    coarse, fine = angle_tables(samples, parts, kdev, low)
    order = row_order(group, frames, first, count)
    piece = (count, 2, feed_dev // 2, LANES)
    shapes = [piece] * parts if split else [(parts, *piece)]
    whole = lambda shape: pl.BlockSpec(shape, lambda i, me_ref: (0,) * len(shape))
    scratch = [
        pltpu.VMEM((parts // 2, samples, 2 * LANES), jnp.bfloat16),
        pltpu.VMEM((steps * order.shape[0], samples), jnp.bfloat16),
    ]
    if split:
        scratch.append(pltpu.VMEM((parts, *piece), jnp.bfloat16))
    result = pl.pallas_call(
        functools.partial(channelise_kernel, low),
        name="channelise",
        grid_spec=pltpu.PrefetchScalarGridSpec(
            num_scalar_prefetch=1,
            grid=(steps,),
            in_specs=[
                whole(coarse.shape),
                whole(fine.shape),
                whole(order.shape),
                pl.BlockSpec((2 * group, frames, samples), lambda i, me_ref: (i, 0, 0)),
            ],
            out_specs=[whole(shape) for shape in shapes],
            scratch_shapes=scratch,
        ),
        out_shape=[jax.ShapeDtypeStruct(shape, jnp.bfloat16) for shape in shapes],
        compiler_params=params(),
        cost_estimate=cost(
            2 * feed_dev * count * samples * (samples + order.shape[1]), 4 * raw.size
        ),
    )(me, jnp.asarray(coarse), jnp.asarray(fine), jnp.asarray(order, jnp.bfloat16), raw)
    return result if split else result[0]


def beam_table(cell_feed, me, parts):
    beams = cell_feed.shape[0]
    cells = beams // 4
    antenna = lax.broadcasted_iota(jnp.int32, (beams, beams), 0)
    cell = lax.broadcasted_iota(jnp.int32, (beams, beams), 1)
    own = beams // parts
    antenna = (me - antenna // own + parts) % parts * own + antenna % own
    place = jnp.sum(jnp.where(cell_feed[None, :] == antenna, cell, 0), axis=1)
    shape = (2, beams, beams)
    part = lax.broadcasted_iota(jnp.int32, shape, 0)
    beam = lax.broadcasted_iota(jnp.int32, shape, 1)
    east = (place // cells)[None, None, :]
    north = (place % cells)[None, None, :]
    quarter = cells // 4
    count = quarter * ((beam // cells) * east) + (beam % cells) * north + quarter * part
    angle = (count % cells).astype(jnp.float32) * (2.0 * math.pi / cells)
    return (jnp.cos(angle) * (1.0 / math.sqrt(cells))).astype(jnp.bfloat16)


def beam_kernel(tile, frames, n_spec, n_prev, me_ref, weight_ref, *refs):
    spec_refs, prev_refs = refs[:n_spec], refs[n_spec : n_spec + n_prev]
    out_ref, right = refs[n_spec + n_prev : n_spec + n_prev + 2]
    pair, pols, group, lanes = spec_refs[0].shape[-4:]
    beams = weight_ref.shape[1]
    parts = weight_ref.shape[2] // group
    half = lanes // 2
    last = len(refs) > n_spec + n_prev + 2
    power, slot = (refs[-1], pl.program_id(0)) if last else (out_ref, 0)
    for d in range(parts):
        for r in range(pair):
            for p in range(pols):
                at = (r * pols + p) * lanes
                if n_spec == 1:
                    block = spec_refs[0][lax.rem(me_ref[0] + (parts - d), parts), r, p]
                else:
                    block = spec_refs[d][r, p]
                right[d * group : (d + 1) * group, at : at + lanes] = block
    lane = lax.broadcasted_iota(jnp.int32, (tile, lanes), 1)
    low = lane < half
    sign = jnp.where(low, -1.0, 1.0)

    for step in range(beams // tile):
        cut_rows = slice(step * tile, (step + 1) * tile)
        first = jnp.dot(weight_ref[0, cut_rows, :], right[...], preferred_element_type=jnp.float32)
        second = jnp.dot(weight_ref[1, cut_rows, :], right[...], preferred_element_type=jnp.float32)
        sums = []
        for r in range(pair):
            total = None
            for p in range(pols):
                cut = slice((r * pols + p) * lanes, (r * pols + p + 1) * lanes)
                turned = pltpu.roll(second[:, cut], half, 1)
                value = first[:, cut] + sign * turned
                total = value * value if total is None else total + value * value
            sums.append(0.125 * (total + pltpu.roll(total, half, 1)))
        power[slot, cut_rows, :] = jnp.where(low, sums[0], sums[1])

    if last:

        @pl.when(pl.program_id(0) == pl.num_programs(0) - 1)
        def _():
            own = out_ref.shape[2]

            def centre(part, carry):
                at = pl.ds(pl.multiple_of(part * own, own), own)
                blocks = [
                    ref[i, at, :] for ref in (*prev_refs, power) for i in range(ref.shape[0])
                ]
                total = functools.reduce(lambda a, b: a + b, blocks)
                mean = (total + pltpu.roll(total, half, 1)) * (1.0 / frames)
                for i, block in enumerate(blocks):
                    out_ref[part, i] = (block - mean).astype(jnp.bfloat16)
                return carry

            lax.fori_loop(0, parts, centre, 0)


def beam_stage(weights, me, arrived, frames, parts, prev=None):
    count, pols, group, lanes = arrived[0].shape[-4:]
    beams = weights.shape[1]
    whole = lambda shape: pl.BlockSpec(shape, lambda i, me_ref: (0,) * len(shape))
    if len(arrived) == 1:
        spec = pl.BlockSpec((parts, 2, pols, group, lanes), lambda i, me_ref: (0, i, 0, 0, 0))
    else:
        spec = pl.BlockSpec((2, pols, group, lanes), lambda i, me_ref: (i, 0, 0, 0))
    scratch = [pltpu.VMEM((parts * group, 2 * pols * lanes), jnp.bfloat16)]
    if prev is None:
        out_shape = jax.ShapeDtypeStruct((count // 2, beams, lanes), jnp.float32)
        out_spec = pl.BlockSpec((1, beams, lanes), lambda i, me_ref: (i, 0, 0))
    else:
        out_shape = jax.ShapeDtypeStruct((parts, frames // 2, beams // parts, lanes), jnp.bfloat16)
        out_spec = whole(out_shape.shape)
        scratch.append(pltpu.VMEM((count // 2, beams, lanes), jnp.float32))
    before = prev or []
    return pl.pallas_call(
        functools.partial(beam_kernel, 256, frames, len(arrived), len(before)),
        name="beams",
        grid_spec=pltpu.PrefetchScalarGridSpec(
            num_scalar_prefetch=1,
            grid=(count // 2,),
            in_specs=[whole(weights.shape)]
            + [spec] * len(arrived)
            + [whole(power.shape) for power in before],
            out_specs=out_spec,
            scratch_shapes=scratch,
        ),
        out_shape=out_shape,
        compiler_params=params(),
        cost_estimate=cost(
            4 * beams * beams * count * pols * lanes, 4 * weights.size + 4 * beams * count * lanes
        ),
    )(me, weights, *arrived, *before)


def turn_value(count, frames):
    folded = jnp.minimum(count, frames - count)
    inner = jnp.minimum(folded, frames // 2 - folded)
    value = jnp.zeros(count.shape, jnp.float32)
    for i in range(frames // 4):
        value = jnp.where(inner == i, np.float32(math.cos(2.0 * math.pi * i / frames)), value)
    return jnp.where(folded > frames // 4, -value, value)


def factor_kernel(frames, delay_ref, out_ref):
    delay = delay_ref[...]
    quarter = frames // 4
    for h in range(1, quarter + 1):
        count = (h * delay) & (frames - 1)
        shifted = (count + (frames - quarter)) & (frames - 1)
        out_ref[2 * h - 2] = turn_value(count, frames).astype(jnp.bfloat16)
        out_ref[2 * h - 1] = turn_value(shifted, frames).astype(jnp.bfloat16)
    out_ref[2 * quarter] = jnp.where((delay & 1) == 1, -1.0, 1.0).astype(jnp.bfloat16)


def factor_stage(delay, frames):
    nfreq, trials = delay.shape
    rows = 32
    terms = frames // 2 + 1
    return pl.pallas_call(
        functools.partial(factor_kernel, frames),
        name="factors",
        grid=(nfreq // rows,),
        in_specs=[pl.BlockSpec((rows, trials), lambda i: (i, 0))],
        out_specs=pl.BlockSpec((terms, rows, trials), lambda i: (0, i, 0)),
        out_shape=jax.ShapeDtypeStruct((terms, nfreq, trials), jnp.bfloat16),
        compiler_params=params(),
        cost_estimate=cost(10 * terms * nfreq * trials, 2 * terms * nfreq * trials),
    )(delay)


def rounded(value):
    return float(np.asarray(value, np.float32).astype(jnp.bfloat16).astype(np.float32))


def turns(count, frames):
    angle = 2.0 * math.pi * (count % frames) / frames
    pair = []
    for value in (math.cos(angle), math.sin(angle)):
        pair.append(float(round(value)) if abs(value - round(value)) < 1e-12 else value)
    return pair


def weighted(terms):
    total = None
    for factor, value in terms:
        if factor == 0.0:
            continue
        term = value if factor == 1.0 else (-value if factor == -1.0 else factor * value)
        total = term if total is None else total + term
    return total


def harmonics_of(values, frames):
    half, quarter = frames // 2, frames // 4
    plus = [values[r] + values[r + half] for r in range(half)]
    minus = [values[r] - values[r + half] for r in range(half)]
    result = []
    for h in range(half + 1):
        base = minus if h % 2 else plus
        real, imag = [(1.0, base[0])], []
        for r in range(1, quarter):
            cosine, sine = (rounded(x) for x in turns(h * r, frames))
            other = base[half - r]
            even = base[r] - other if h % 2 else base[r] + other
            odd = base[r] + other if h % 2 else base[r] - other
            real.append((cosine, even))
            imag.append((-sine, odd))
        cosine, sine = (rounded(x) for x in turns(h * quarter, frames))
        real.append((cosine, base[quarter]))
        imag.append((-sine, base[quarter]))
        result.append((weighted(real), weighted(imag)))
    return result


def dedisperse_kernel(frames, nfreq, arrived_ref, factor_ref, out_ref, left, zero):
    srcs, pairs, own, lanes = arrived_ref.shape
    half = frames // 2
    tile = factor_ref.shape[2]

    @pl.when(pl.program_id(0) == 0)
    def _():
        low = lax.broadcasted_iota(jnp.int32, (own, lanes), 1) < lanes // 2
        zero[...] = jnp.zeros_like(zero)

        def one(j, carry):
            values = []
            for i in range(pairs):
                even = arrived_ref[2 * j, i].astype(jnp.float32)
                odd = arrived_ref[2 * j + 1, i].astype(jnp.float32)
                values.append(jnp.where(low, even, pltpu.roll(odd, lanes // 2, 1)))
                values.append(jnp.where(low, pltpu.roll(even, lanes // 2, 1), odd))
            parts = harmonics_of(values, frames)
            zero[...] += parts[0][0].astype(jnp.bfloat16).astype(jnp.float32)
            for h in range(1, half + 1):
                left[j, h - 1, :own, :] = parts[h][0].astype(jnp.bfloat16)
                if h < half:
                    left[j, h - 1, own:, :] = parts[h][1].astype(jnp.bfloat16)
            return carry

        lax.fori_loop(0, srcs // 2, one, 0)

    scale = 1.0 / (frames * math.sqrt(nfreq))
    first = scale * jnp.sum(zero[...], axis=1, keepdims=True)
    real, imag = [], []
    quarter = frames // 4
    parity = factor_ref[2 * quarter]
    for h in range(1, half):
        block = jnp.concatenate([left[j, h - 1] for j in range(srcs // 2)], axis=1)
        base = min(h, half - h)
        cosines, sines = factor_ref[2 * base - 2], factor_ref[2 * base - 1]
        if h > quarter:
            cosines, sines = cosines * parity, sines * -parity
        by_cos = jnp.dot(block, cosines, preferred_element_type=jnp.float32)
        by_sin = jnp.dot(block, sines, preferred_element_type=jnp.float32)
        real.append((2.0 * scale) * (by_cos[:own] - by_sin[own:]))
        imag.append((2.0 * scale) * (by_sin[:own] + by_cos[own:]))
    block = jnp.concatenate([left[j, half - 1, :own, :] for j in range(srcs // 2)], axis=1)
    last = scale * jnp.dot(block, parity, preferred_element_type=jnp.float32)
    for t in range(half):
        parts = []
        for parity in range(2):
            terms = []
            for h in range(2 - parity, half, 2):
                cosine, sine = turns(h * t, frames)
                terms.append((cosine, real[h - 1]))
                terms.append((-sine, imag[h - 1]))
            parts.append(weighted(terms))
        even = parts[0] + first + (last if t % 2 == 0 else -last)
        out_ref[:, t, :] = even + parts[1]
        out_ref[:, t + half, :] = even - parts[1]


def dedisperse_stage(arrived, factors, frames):
    srcs, pairs, own, lanes = arrived.shape
    terms, nfreq, trials = factors.shape
    tile = 2 * LANES
    return pl.pallas_call(
        functools.partial(dedisperse_kernel, frames, nfreq),
        name="dedisperse",
        grid=(trials // tile,),
        in_specs=[
            pl.BlockSpec(arrived.shape, lambda i: (0, 0, 0, 0)),
            pl.BlockSpec((terms, nfreq, tile), lambda i: (0, 0, i)),
        ],
        out_specs=pl.BlockSpec((own, frames, tile), lambda i: (0, 0, i)),
        out_shape=jax.ShapeDtypeStruct((own, frames, trials), jnp.float32),
        scratch_shapes=[
            pltpu.VMEM((srcs // 2, frames // 2, 2 * own, lanes), jnp.bfloat16),
            pltpu.VMEM((own, lanes), jnp.float32),
        ],
        compiler_params=params(),
        cost_estimate=cost(8 * own * terms * nfreq * trials, 2 * factors.size + 4 * own * frames * trials),
    )(arrived, factors)


def chunks_of(frames):
    end = max(2, frames // 4)
    return ((0, end, False), (end, frames - 2 * end, True), (frames - end, end, False))


def exchange(message, parts):
    if not isinstance(message, (list, tuple)):
        return [lax.all_to_all(message, "wide", split_axis=0, concat_axis=0, tiled=True)]
    arrived = [message[0]]
    for d in range(1, parts):
        ring = [(i, (i + d) % parts) for i in range(parts)]
        arrived.append(lax.ppermute(message[d], "wide", ring))
    return arrived


def tiled_body(parts, raw, cell_feed, dm_delay):
    feed_dev, frames, samples = raw.shape
    me = lax.axis_index("wide").astype(jnp.int32)
    own, none = me.reshape(1), jnp.zeros((1,), jnp.int32)
    cuts = chunks_of(frames)
    messages = []
    for first, count, split in cuts:
        message = channelise(raw, own if split else none, first, count, parts, split)
        raw, cell_feed, dm_delay, message = lax.optimization_barrier(
            (raw, cell_feed, dm_delay, message)
        )
        messages.append(message)
    weights = beam_table(cell_feed, me, parts)
    factors = factor_stage(jnp.transpose(dm_delay), frames)
    powers = []
    for message in messages[:-1]:
        power = beam_stage(weights, own, exchange(message, parts), frames, parts)
        weights, power = lax.optimization_barrier((weights, power))
        powers.append(power)
    centred = beam_stage(weights, own, exchange(messages[-1], parts), frames, parts, powers)
    arrived = lax.all_to_all(centred, "wide", split_axis=0, concat_axis=0, tiled=True)
    return dedisperse_stage(arrived, factors, frames)


def fits(parts, raw_shape, cells, delay_shape):
    feed_dev, frames, samples = raw_shape
    trials, nfreq = delay_shape
    return (
        samples // parts == LANES
        and nfreq * 2 == samples
        and samples % (2 * LANES) == 0
        and feed_dev % 32 == 0
        and frames % 16 == 0
        and frames & (frames - 1) == 0
        and cells % (256) == 0
        and cells // parts == LANES // 2
        and trials % (2 * LANES) == 0
        and parts % 2 == 0
    )


def solution(mesh):
    parts = mesh.shape["wide"]

    def body(raw, cell_feed, dm_delay):
        if fits(parts, raw.shape, cell_feed.shape[0], dm_delay.shape):
            return tiled_body(parts, raw, cell_feed, dm_delay)
        return plain_body(raw, cell_feed, dm_delay)

    placed = (P(("grp", "wide"), None, None), P(), P())
    return jax.shard_map(
        body, mesh=mesh, in_specs=placed, out_specs=P(("grp", "wide"), None, None), check_vma=False
    )
```

```python
import functools
import math

import jax
import jax.numpy as jnp
import numpy as np
from jax import lax
from jax.experimental import pallas as pl
from jax.experimental.pallas import tpu as pltpu
from jax.sharding import PartitionSpec as P

LANES = 128
VMEM_LIMIT = 60000 * 1024

EAST_COSINE = np.array([[1, 1, 1, 1], [1, 0, -1, 0], [1, -1, 1, -1], [1, 0, -1, 0]], np.float32)
EAST_SINE = np.array([[0, 0, 0, 0], [0, 1, 0, -1], [0, 0, 0, 0], [0, -1, 0, 1]], np.float32)


def phase_pair(count, length):
    angle = (count % length).astype(jnp.float32) * (2.0 * math.pi / length)
    return (jnp.cos(angle), jnp.sin(angle))


def channel_table(samples, width):
    sample_ids = lax.broadcasted_iota(jnp.int32, (samples, width), 0)
    freq_ids = lax.broadcasted_iota(jnp.int32, (samples, width), 1)
    cosine, sine = phase_pair(sample_ids * freq_ids, samples)
    factor = 1.0 / math.sqrt(samples)
    return jnp.concatenate([cosine * factor, -sine * factor], axis=1).astype(jnp.bfloat16)


def sky_table(cells):
    rows = lax.broadcasted_iota(jnp.int32, (cells, cells), 0)
    cols = lax.broadcasted_iota(jnp.int32, (cells, cells), 1)
    cosine, sine = phase_pair(rows * cols, cells)
    real_row = jnp.stack([cosine, sine], axis=-1)
    imag_row = jnp.stack([-sine, cosine], axis=-1)
    factor = 1.0 / math.sqrt(cells)
    return (jnp.stack([real_row, imag_row], axis=1) * factor).astype(jnp.bfloat16)


def transform_table(frames):
    terms = frames // 2 + 1
    harmonic = lax.broadcasted_iota(jnp.int32, (terms, frames), 0)
    moment = lax.broadcasted_iota(jnp.int32, (terms, frames), 1)
    cosine, sine = phase_pair(harmonic * moment, frames)
    return jnp.stack([cosine, -sine]).astype(jnp.bfloat16)


def beam_power(spec, feed_index, table):
    grid = jnp.take(spec, feed_index.reshape(-1), axis=0)
    grid = grid.reshape(feed_index.shape + spec.shape[1:])
    beams = jnp.einsum("joni,penrif->poerfj", table, grid, preferred_element_type=jnp.float32)
    real_part = beams[:, 0]
    imag_part = beams[:, 1]
    cosines = jnp.asarray(EAST_COSINE)
    sines = jnp.asarray(EAST_SINE)
    high = lax.Precision.HIGHEST
    east_real = 0.5 * (
        jnp.einsum("qe,perfj->prfqj", cosines, real_part, precision=high)
        + jnp.einsum("qe,perfj->prfqj", sines, imag_part, precision=high)
    )
    east_imag = 0.5 * (
        jnp.einsum("qe,perfj->prfqj", cosines, imag_part, precision=high)
        - jnp.einsum("qe,perfj->prfqj", sines, real_part, precision=high)
    )
    power = 0.5 * jnp.sum(east_real * east_real + east_imag * east_imag, axis=0)
    return power.reshape(power.shape[0], power.shape[1], -1)


def dedisperse(spectrum, dm_delay, frames):
    base_cos, base_sin = phase_pair(jnp.transpose(dm_delay), frames)
    beams_dev = spectrum.shape[3]
    nfreq = spectrum.shape[2]

    def one_term(carry, block):
        cosine, sine = carry
        cos_half = cosine.astype(jnp.bfloat16)
        sin_half = sine.astype(jnp.bfloat16)
        upper = jnp.concatenate([cos_half, sin_half], axis=1)
        lower = jnp.concatenate([-sin_half, cos_half], axis=1)
        right = jnp.concatenate([upper, lower], axis=0)
        left = block.reshape(2 * nfreq, beams_dev)
        result = lax.dot_general(
            left, right, (((0,), (0,)), ((), ())), preferred_element_type=jnp.float32
        )
        next_cos = cosine * base_cos - sine * base_sin
        next_sin = sine * base_cos + cosine * base_sin
        return ((next_cos, next_sin), result)

    start = (jnp.ones(base_cos.shape, jnp.float32), jnp.zeros(base_cos.shape, jnp.float32))
    final, trials = lax.scan(one_term, start, spectrum)
    return trials.reshape(trials.shape[0], beams_dev, 2, -1)


def synthesis(trials, frames, nfreq):
    terms = frames // 2 + 1
    moment = lax.broadcasted_iota(jnp.int32, (frames, terms), 0)
    harmonic = lax.broadcasted_iota(jnp.int32, (frames, terms), 1)
    cosine, sine = phase_pair(moment * harmonic, frames)
    weight = jnp.where((harmonic == 0) | (harmonic * 2 == frames), 1.0, 2.0).astype(jnp.float32)
    weight = weight / (frames * math.sqrt(nfreq))
    table = jnp.stack([cosine * weight, -sine * weight], axis=1)
    return jnp.einsum("tuk,kbud->btd", table, trials, precision=lax.Precision.HIGHEST)


def plain_body(raw, cell_feed, dm_delay):
    feed_dev, frames, samples = raw.shape
    nfreq = samples // 2
    table = channel_table(samples, nfreq)
    spectra = jnp.dot(
        raw.reshape(feed_dev * frames, samples), table, preferred_element_type=jnp.float32
    )
    spectra = spectra.astype(jnp.bfloat16).reshape(feed_dev, frames, 2, nfreq)
    cells = cell_feed.shape[0] // 4
    polar = lax.broadcasted_iota(jnp.int32, (2, 4, cells), 0)
    feed_index = 2 * cell_feed.reshape(1, 4, cells) + polar
    table_sky = sky_table(cells)
    arrived = lax.all_to_all(spectra, "wide", split_axis=3, concat_axis=0, tiled=True)
    power = beam_power(arrived, feed_index, table_sky)
    centred = (power - jnp.mean(power, axis=0, keepdims=True)).astype(jnp.bfloat16)
    time_table = transform_table(frames)
    local = jnp.einsum("okr,rfb->kofb", time_table, centred, preferred_element_type=jnp.float32)
    spectrum = lax.all_to_all(
        local.astype(jnp.bfloat16), "wide", split_axis=3, concat_axis=2, tiled=True
    )
    trials = dedisperse(spectrum, dm_delay, frames)
    return synthesis(trials, frames, nfreq)


def params(steps=1):
    return pltpu.CompilerParams(
        dimension_semantics=("arbitrary",) * steps, vmem_limit_bytes=VMEM_LIMIT
    )


def cost(flops, nbytes):
    return pl.CostEstimate(flops=int(flops), bytes_accessed=int(nbytes), transcendentals=0)


def angle_tables(samples, parts, kdev, low):
    freq = np.arange(parts)[:, None] * kdev + np.tile(np.arange(kdev), 2)[None, :]
    quarter = np.repeat(np.arange(2), kdev) * (samples // 4)
    coarse = np.arange(0, samples, low)[None, :, None] * freq[:, None, :] % samples
    fine = (np.arange(low)[None, :, None] * freq[:, None, :] + quarter) % samples
    turn = 2.0 * np.pi / samples
    factor = 1.0 / math.sqrt(samples)
    first = np.stack([np.cos(coarse * turn), np.sin(coarse * turn)])
    second = np.stack([np.cos(fine * turn), np.sin(fine * turn)]) * factor
    return first.astype(np.float32), second.astype(np.float32)


def channelise_kernel(low, begin, frames, me_ref, coarse_ref, fine_ref, raw_ref, *refs):
    split = len(refs) > 4
    out_refs = refs[:-4] if split else refs[:1]
    table, rows, order = refs[-4:-1] if split else refs[1:]
    out_ref = refs[-1] if split else refs[0]
    slots, samples, wide_cols = table.shape
    parts, count, pols, antennas, lanes = out_ref.shape
    own = order.shape[0]
    steps = rows.shape[0] // own
    group = antennas // steps
    pairs = parts // 2
    step = pl.program_id(0)

    def make(pair, slot):
        for side in range(2):
            part = 2 * pair + side
            fine_cos, fine_sin = fine_ref[0, part], fine_ref[1, part]
            for block in range(samples // low):
                cos_a = coarse_ref[0, part, block : block + 1, :]
                sin_a = coarse_ref[1, part, block : block + 1, :]
                value = cos_a * fine_cos - sin_a * fine_sin
                table[slot, block * low : (block + 1) * low, side * lanes : (side + 1) * lanes] = (
                    value.astype(jnp.bfloat16)
                )

    @pl.when(step == 0)
    def _():
        line = lax.broadcasted_iota(jnp.int32, order.shape, 0)
        column = lax.broadcasted_iota(jnp.int32, order.shape, 1)
        bits, pol_bits = group.bit_length() - 1, pols.bit_length() - 1
        antenna, pol = line & (group - 1), (line >> bits) & (pols - 1)
        wanted = (antenna * pols + pol) * frames + begin + (line >> (bits + pol_bits))
        order[...] = jnp.where(wanted == column, 1.0, 0.0).astype(jnp.bfloat16)
        make(0, 0)

    source = raw_ref[...].reshape(-1, samples)
    ordered = jnp.dot(order[...], source, preferred_element_type=jnp.float32)
    rows[pl.ds(pl.multiple_of(step * own, own), own), :] = ordered.astype(jnp.bfloat16)

    def use(pair, slot):
        value = jnp.dot(rows[...], table[slot], preferred_element_type=jnp.float32)
        value = value.astype(jnp.bfloat16)
        for side in range(2):
            for i in range(steps):
                block = value[i * own : (i + 1) * own, side * lanes : (side + 1) * lanes]
                out_ref[2 * pair + side, :, :, i * group : (i + 1) * group, :] = block.reshape(
                    count, pols, group, lanes
                )

    @pl.when(step == steps - 1)
    def _():
        def one(twice, carry):
            for slot in range(2):
                pair = 2 * twice + slot
                make(lax.rem(pair + 1, pairs), 1 - slot)
                use(pair, slot)
            return carry

        lax.fori_loop(0, pairs // 2, one, 0)
        if split:
            for part in range(parts):
                out_refs[part][...] = out_ref[lax.rem(me_ref[0] + part, parts)]


def channelise(raw, me, first, count, parts, split):
    feed_dev, frames, samples = raw.shape
    kdev = samples // 2 // parts
    low = 64
    group = 16
    steps = feed_dev // (2 * group)
    coarse, fine = angle_tables(samples, parts, kdev, low)
    own = 2 * group * count
    piece = (count, 2, feed_dev // 2, LANES)
    shapes = [piece] * parts if split else [(parts, *piece)]
    whole = lambda shape: pl.BlockSpec(shape, lambda i, me_ref: (0,) * len(shape))
    scratch = [
        pltpu.VMEM((2, samples, 2 * LANES), jnp.bfloat16),
        pltpu.VMEM((steps * own, samples), jnp.bfloat16),
        pltpu.VMEM((own, 2 * group * frames), jnp.bfloat16),
    ]
    if split:
        scratch.append(pltpu.VMEM((parts, *piece), jnp.bfloat16))
    result = pl.pallas_call(
        functools.partial(channelise_kernel, low, first, frames),
        name="channelise",
        grid_spec=pltpu.PrefetchScalarGridSpec(
            num_scalar_prefetch=1,
            grid=(steps,),
            in_specs=[
                whole(coarse.shape),
                whole(fine.shape),
                pl.BlockSpec((2 * group, frames, samples), lambda i, me_ref: (i, 0, 0)),
            ],
            out_specs=[whole(shape) for shape in shapes],
            scratch_shapes=scratch,
        ),
        out_shape=[jax.ShapeDtypeStruct(shape, jnp.bfloat16) for shape in shapes],
        compiler_params=params(),
        cost_estimate=cost(
            2 * feed_dev * count * samples * samples, 4 * raw.size
        ),
    )(me, jnp.asarray(coarse), jnp.asarray(fine), raw)
    return result if split else result[0]


def beam_table(cell_feed, me, parts):
    beams = cell_feed.shape[0]
    cells = beams // 4
    own = beams // parts
    antenna = lax.broadcasted_iota(jnp.int32, (beams, beams), 0)
    cell = lax.broadcasted_iota(jnp.int32, (beams, beams), 1)
    antenna = (me - antenna // own + parts) % parts * own + antenna % own
    place = jnp.sum(jnp.where(cell_feed[None, :] == antenna, cell, 0), axis=1)
    east, north = place // cells, place % cells
    count = lax.broadcasted_iota(jnp.int32, (cells, beams), 0) * north[None, :]
    cosine, sine = phase_pair(count, cells)
    factor = 1.0 / math.sqrt(cells)
    cosine = (cosine * factor).astype(jnp.bfloat16)
    sine = (sine * factor).astype(jnp.bfloat16)
    cosine, sine = lax.optimization_barrier((cosine, sine))
    quarters = jnp.arange(4, dtype=jnp.int32)[:, None, None] * east % 4
    odd, minus = quarters % 2 == 1, quarters >= 2
    real = jnp.where(odd, -sine, cosine)
    imag = jnp.where(odd, -cosine, -sine)
    table = jnp.stack([jnp.where(minus, -real, real), jnp.where(minus, -imag, imag)])
    return table.reshape(2, beams, beams)


def beam_kernel(frames, n_spec, n_prev, me_ref, weight_ref, *refs):
    spec_refs, prev_refs = refs[:n_spec], refs[n_spec : n_spec + n_prev]
    out_refs, right = refs[n_spec + n_prev : -1], refs[-1]
    last = len(out_refs) > 1
    count, pols, group, lanes = spec_refs[0].shape[-4:]
    tile = weight_ref.shape[1]
    parts = weight_ref.shape[2] // group
    half = lanes // 2
    pairs = count // 2

    @pl.when(pl.program_id(0) == 0)
    def _():
        for d in range(parts):
            for r in range(count):
                for p in range(pols):
                    at = (r % 2 * pols + p) * lanes
                    if n_spec == 1:
                        block = spec_refs[0][lax.rem(me_ref[0] + (parts - d), parts), r, p]
                    else:
                        block = spec_refs[d][r, p]
                    right[r // 2, d * group : (d + 1) * group, at : at + lanes] = block

    low = lax.broadcasted_iota(jnp.int32, (tile, lanes), 1) < half
    sign = jnp.where(low, -1.0, 1.0)

    def power_of(pair):
        first = jnp.dot(weight_ref[0], right[pair], preferred_element_type=jnp.float32)
        second = jnp.dot(weight_ref[1], right[pair], preferred_element_type=jnp.float32)
        sums = []
        for r in range(2):
            total = None
            for p in range(pols):
                cut = slice((r * pols + p) * lanes, (r * pols + p + 1) * lanes)
                turned = pltpu.roll(second[:, cut], half, 1)
                value = first[:, cut] + sign * turned
                total = value * value if total is None else total + value * value
            sums.append(0.125 * (total + pltpu.roll(total, half, 1)))
        return jnp.where(low, sums[0], sums[1])

    if not last:

        def one(pair, carry):
            out_refs[0][pair] = power_of(pair)
            return carry

        lax.fori_loop(0, pairs, one, 0)

    if last:
        powers = [power_of(pair) for pair in range(pairs)]
        blocks = [ref[i] for ref in prev_refs for i in range(ref.shape[0])] + powers
        total = functools.reduce(lambda a, b: a + b, blocks)
        mean = (total + pltpu.roll(total, half, 1)) * (1.0 / frames)
        hold = out_refs[parts]
        own = hold.shape[2]
        per = tile // own
        at = pl.program_id(0) * per
        for i, block in enumerate(blocks):
            hold[pl.ds(at, per), i] = (block - mean).astype(jnp.bfloat16).reshape(per, own, lanes)

        @pl.when(pl.program_id(0) == pl.num_programs(0) - 1)
        def _():
            for part in range(parts):
                out_refs[part][...] = hold[lax.rem(me_ref[0] + part, parts)]


def beam_stage(weights, me, arrived, frames, parts, prev=None):
    count, pols, group, lanes = arrived[0].shape[-4:]
    beams = weights.shape[1]
    tile = 256
    whole = lambda shape: pl.BlockSpec(shape, lambda i, me_ref: (0,) * len(shape))
    rows = lambda power: pl.BlockSpec((power.shape[0], tile, lanes), lambda i, me_ref: (0, i, 0))
    scratch = [pltpu.VMEM((count // 2, parts * group, 2 * pols * lanes), jnp.bfloat16)]
    before = prev or []
    if prev is None:
        out_shape = [jax.ShapeDtypeStruct((count // 2, beams, lanes), jnp.float32)]
        out_specs = [rows(out_shape[0])]
    else:
        piece = (frames // 2, beams // parts, lanes)
        out_shape = [jax.ShapeDtypeStruct(piece, jnp.bfloat16)] * parts
        out_specs = [whole(piece)] * parts
        scratch.insert(0, pltpu.VMEM((parts, *piece), jnp.bfloat16))
    result = pl.pallas_call(
        functools.partial(beam_kernel, frames, len(arrived), len(before)),
        name="beams",
        grid_spec=pltpu.PrefetchScalarGridSpec(
            num_scalar_prefetch=1,
            grid=(beams // tile,),
            in_specs=[pl.BlockSpec((2, tile, beams), lambda i, me_ref: (0, i, 0))]
            + [whole(piece.shape) for piece in arrived]
            + [rows(power) for power in before],
            out_specs=out_specs,
            scratch_shapes=scratch,
        ),
        out_shape=out_shape,
        compiler_params=params(),
        cost_estimate=cost(
            4 * beams * beams * count * pols * lanes, 4 * weights.size + 4 * beams * count * lanes
        ),
    )(me, weights, *arrived, *before)
    return result[0] if prev is None else result


def turn_value(count, frames):
    folded = jnp.minimum(count, frames - count)
    inner = jnp.minimum(folded, frames // 2 - folded)
    value = jnp.zeros(count.shape, jnp.float32)
    for i in range(frames // 4):
        value = jnp.where(inner == i, np.float32(math.cos(2.0 * math.pi * i / frames)), value)
    return jnp.where(folded > frames // 4, -value, value)


def factor_kernel(frames, delay_ref, out_ref):
    delay = delay_ref[...]
    quarter = frames // 4
    for h in range(1, quarter + 1):
        count = (h * delay) & (frames - 1)
        shifted = (count + (frames - quarter)) & (frames - 1)
        out_ref[2 * h - 2] = turn_value(count, frames).astype(jnp.bfloat16)
        out_ref[2 * h - 1] = turn_value(shifted, frames).astype(jnp.bfloat16)
    out_ref[2 * quarter] = jnp.where((delay & 1) == 1, -1.0, 1.0).astype(jnp.bfloat16)


def factor_stage(delay, frames):
    nfreq, trials = delay.shape
    rows = 32
    terms = frames // 2 + 1
    return pl.pallas_call(
        functools.partial(factor_kernel, frames),
        name="factors",
        grid=(nfreq // rows,),
        in_specs=[pl.BlockSpec((rows, trials), lambda i: (i, 0))],
        out_specs=pl.BlockSpec((terms, rows, trials), lambda i: (0, i, 0)),
        out_shape=jax.ShapeDtypeStruct((terms, nfreq, trials), jnp.bfloat16),
        compiler_params=params(),
        cost_estimate=cost(10 * terms * nfreq * trials, 2 * terms * nfreq * trials),
    )(delay)


def rounded(value):
    return float(np.asarray(value, np.float32).astype(jnp.bfloat16).astype(np.float32))


def turns(count, frames):
    angle = 2.0 * math.pi * (count % frames) / frames
    pair = []
    for value in (math.cos(angle), math.sin(angle)):
        pair.append(float(round(value)) if abs(value - round(value)) < 1e-12 else value)
    return pair


def weighted(terms):
    total = None
    for factor, value in terms:
        if factor == 0.0:
            continue
        term = value if factor == 1.0 else (-value if factor == -1.0 else factor * value)
        total = term if total is None else total + term
    return total


def harmonics_of(values, frames):
    half, quarter = frames // 2, frames // 4
    plus = [values[r] + values[r + half] for r in range(half)]
    minus = [values[r] - values[r + half] for r in range(half)]
    result = []
    for h in range(half + 1):
        base = minus if h % 2 else plus
        real, imag = [(1.0, base[0])], []
        for r in range(1, quarter):
            cosine, sine = (rounded(x) for x in turns(h * r, frames))
            other = base[half - r]
            even = base[r] - other if h % 2 else base[r] + other
            odd = base[r] + other if h % 2 else base[r] - other
            real.append((cosine, even))
            imag.append((-sine, odd))
        cosine, sine = (rounded(x) for x in turns(h * quarter, frames))
        real.append((cosine, base[quarter]))
        imag.append((-sine, base[quarter]))
        result.append((weighted(real), weighted(imag)))
    return result


def dedisperse_kernel(frames, nfreq, me_ref, *refs):
    arrived_refs, (factors_ref, out_ref, held, left, zero, slots, sems) = refs[:-7], refs[-7:]
    parts = len(arrived_refs)
    pairs, own, lanes = arrived_refs[0].shape
    half, quarter = frames // 2, frames // 4
    step, steps = pl.program_id(0), pl.num_programs(0)
    tile = slots.shape[3]

    def fetch(at, slot):
        cut = pl.ds(pl.multiple_of(at * tile, tile), tile)
        return pltpu.make_async_copy(factors_ref.at[:, :, cut], slots.at[slot], sems.at[slot])

    @pl.when(step == 0)
    def _():
        fetch(0, 0).start()
        low = lax.broadcasted_iota(jnp.int32, (own, lanes), 1) < lanes // 2
        zero[...] = jnp.zeros_like(zero)
        for d in range(parts):
            held[lax.rem(me_ref[0] + (parts - d), parts)] = arrived_refs[d][...]

        def one(j, carry):
            values = []
            for i in range(pairs):
                even = held[2 * j, i].astype(jnp.float32)
                odd = held[2 * j + 1, i].astype(jnp.float32)
                values.append(jnp.where(low, even, pltpu.roll(odd, lanes // 2, 1)))
                values.append(jnp.where(low, pltpu.roll(even, lanes // 2, 1), odd))
            terms = harmonics_of(values, frames)
            zero[...] += terms[0][0].astype(jnp.bfloat16).astype(jnp.float32)
            for h in range(1, half + 1):
                left[j, h - 1, :own, :] = terms[h][0].astype(jnp.bfloat16)
                if h < half:
                    left[j, h - 1, own:, :] = terms[h][1].astype(jnp.bfloat16)
            return carry

        lax.fori_loop(0, parts // 2, one, 0)

    slot = lax.rem(step, 2)

    @pl.when(step + 1 < steps)
    def _():
        fetch(step + 1, 1 - slot).start()

    fetch(step, slot).wait()
    factor_ref = slots.at[slot]
    scale = 1.0 / (frames * math.sqrt(nfreq))
    first = scale * jnp.sum(zero[...], axis=1, keepdims=True)
    real, imag = [], []
    parity = factor_ref[2 * quarter]
    for h in range(1, half):
        block = jnp.concatenate([left[j, h - 1] for j in range(parts // 2)], axis=1)
        base = min(h, half - h)
        cosines, sines = factor_ref[2 * base - 2], factor_ref[2 * base - 1]
        if h > quarter:
            cosines, sines = cosines * parity, sines * -parity
        by_cos = jnp.dot(block, cosines, preferred_element_type=jnp.float32)
        by_sin = jnp.dot(block, sines, preferred_element_type=jnp.float32)
        real.append((2.0 * scale) * (by_cos[:own] - by_sin[own:]))
        imag.append((2.0 * scale) * (by_sin[:own] + by_cos[own:]))
    block = jnp.concatenate([left[j, half - 1, :own, :] for j in range(parts // 2)], axis=1)
    last = scale * jnp.dot(block, parity, preferred_element_type=jnp.float32)
    for t in range(half):
        sums = []
        for odd in range(2):
            terms = []
            for h in range(2 - odd, half, 2):
                cosine, sine = turns(h * t, frames)
                terms.append((cosine, real[h - 1]))
                terms.append((-sine, imag[h - 1]))
            sums.append(weighted(terms))
        even = sums[0] + first + (last if t % 2 == 0 else -last)
        out_ref[:, t, :] = even + sums[1]
        out_ref[:, t + half, :] = even - sums[1]


def dedisperse_stage(me, arrived, factors, frames):
    pairs, own, lanes = arrived[0].shape
    parts = len(arrived)
    terms, nfreq, trials = factors.shape
    tile = 2 * LANES
    whole = lambda shape: pl.BlockSpec(shape, lambda i, me_ref: (0,) * len(shape))
    return pl.pallas_call(
        functools.partial(dedisperse_kernel, frames, nfreq),
        name="dedisperse",
        grid_spec=pltpu.PrefetchScalarGridSpec(
            num_scalar_prefetch=1,
            grid=(trials // tile,),
            in_specs=[whole(piece.shape) for piece in arrived]
            + [pl.BlockSpec(memory_space=pl.ANY)],
            out_specs=pl.BlockSpec((own, frames, tile), lambda i, me_ref: (0, 0, i)),
            scratch_shapes=[
                pltpu.VMEM((parts, pairs, own, lanes), jnp.bfloat16),
                pltpu.VMEM((parts // 2, frames // 2, 2 * own, lanes), jnp.bfloat16),
                pltpu.VMEM((own, lanes), jnp.float32),
                pltpu.VMEM((2, terms, nfreq, tile), jnp.bfloat16),
                pltpu.SemaphoreType.DMA((2,)),
            ],
        ),
        out_shape=jax.ShapeDtypeStruct((own, frames, trials), jnp.float32),
        compiler_params=params(),
        cost_estimate=cost(
            8 * own * terms * nfreq * trials, 2 * factors.size + 4 * own * frames * trials
        ),
    )(me, *arrived, factors)


def chunks_of(frames):
    end = max(2, frames // 4)
    return ((0, end, False), (end, frames - 2 * end, True), (frames - end, end, False))


def exchange(message, parts):
    if not isinstance(message, (list, tuple)):
        return [lax.all_to_all(message, "wide", split_axis=0, concat_axis=0, tiled=True)]
    arrived = [message[0]]
    for d in range(1, parts):
        ring = [(i, (i + d) % parts) for i in range(parts)]
        arrived.append(lax.ppermute(message[d], "wide", ring))
    return arrived


def tiled_body(parts, raw, cell_feed, dm_delay):
    feed_dev, frames, samples = raw.shape
    me = lax.axis_index("wide").astype(jnp.int32)
    own = me.reshape(1)
    cuts = chunks_of(frames)
    messages = []
    for first, count, split in cuts:
        message = channelise(raw, own, first, count, parts, split)
        raw, cell_feed, dm_delay, message = lax.optimization_barrier(
            (raw, cell_feed, dm_delay, message)
        )
        messages.append(message)
    weights = beam_table(cell_feed, me, parts)
    factors = factor_stage(jnp.transpose(dm_delay), frames)
    powers = []
    for message in messages[:-1]:
        power = beam_stage(weights, own, exchange(message, parts), frames, parts)
        weights, power = lax.optimization_barrier((weights, power))
        powers.append(power)
    weights, factors = lax.optimization_barrier((weights, factors))
    centred = beam_stage(weights, own, exchange(messages[-1], parts), frames, parts, powers)
    return dedisperse_stage(own, exchange(centred, parts), factors, frames)


def fits(parts, raw_shape, cells, delay_shape):
    feed_dev, frames, samples = raw_shape
    trials, nfreq = delay_shape
    return (
        samples // parts == LANES
        and nfreq * 2 == samples
        and samples % (2 * LANES) == 0
        and feed_dev % 32 == 0
        and frames % 16 == 0
        and frames & (frames - 1) == 0
        and cells % (256) == 0
        and cells // parts == LANES // 2
        and trials % (2 * LANES) == 0
        and parts % 4 == 0
    )


def solution(mesh):
    parts = mesh.shape["wide"]

    def body(raw, cell_feed, dm_delay):
        if fits(parts, raw.shape, cell_feed.shape[0], dm_delay.shape):
            return tiled_body(parts, raw, cell_feed, dm_delay)
        return plain_body(raw, cell_feed, dm_delay)

    placed = (P(("grp", "wide"), None, None), P(), P())
    return jax.shard_map(
        body, mesh=mesh, in_specs=placed, out_specs=P(("grp", "wide"), None, None), check_vma=False
    )
```

```python
import functools
import math

import jax
import jax.numpy as jnp
import numpy as np
from jax import lax
from jax.experimental import pallas as pl
from jax.experimental.pallas import tpu as pltpu
from jax.sharding import PartitionSpec as P


LANES = 128
VMEM_LIMIT = 58 * 1024 * 1024

EAST_COSINE = np.array([[1, 1, 1, 1], [1, 0, -1, 0], [1, -1, 1, -1], [1, 0, -1, 0]], np.float32)
EAST_SINE = np.array([[0, 0, 0, 0], [0, 1, 0, -1], [0, 0, 0, 0], [0, -1, 0, 1]], np.float32)


def phase_pair(count, length):
    angle = (count % length).astype(jnp.float32) * (2.0 * math.pi / length)
    return (jnp.cos(angle), jnp.sin(angle))


def channel_table(samples, width):
    sample_ids = lax.broadcasted_iota(jnp.int32, (samples, width), 0)
    freq_ids = lax.broadcasted_iota(jnp.int32, (samples, width), 1)
    cosine, sine = phase_pair(sample_ids * freq_ids, samples)
    factor = 1.0 / math.sqrt(samples)
    return jnp.concatenate([cosine * factor, -sine * factor], axis=1).astype(jnp.bfloat16)


def sky_table(cells):
    rows = lax.broadcasted_iota(jnp.int32, (cells, cells), 0)
    cols = lax.broadcasted_iota(jnp.int32, (cells, cells), 1)
    cosine, sine = phase_pair(rows * cols, cells)
    real_row = jnp.stack([cosine, sine], axis=-1)
    imag_row = jnp.stack([-sine, cosine], axis=-1)
    factor = 1.0 / math.sqrt(cells)
    return (jnp.stack([real_row, imag_row], axis=1) * factor).astype(jnp.bfloat16)


def transform_table(frames):
    terms = frames // 2 + 1
    harmonic = lax.broadcasted_iota(jnp.int32, (terms, frames), 0)
    moment = lax.broadcasted_iota(jnp.int32, (terms, frames), 1)
    cosine, sine = phase_pair(harmonic * moment, frames)
    return jnp.stack([cosine, -sine]).astype(jnp.bfloat16)


def beam_power(spec, feed_index, table):
    grid = jnp.take(spec, feed_index.reshape(-1), axis=0)
    grid = grid.reshape(feed_index.shape + spec.shape[1:])
    beams = jnp.einsum("joni,penrif->poerfj", table, grid, preferred_element_type=jnp.float32)
    real_part = beams[:, 0]
    imag_part = beams[:, 1]
    cosines = jnp.asarray(EAST_COSINE)
    sines = jnp.asarray(EAST_SINE)
    high = lax.Precision.HIGHEST
    east_real = 0.5 * (
        jnp.einsum("qe,perfj->prfqj", cosines, real_part, precision=high)
        + jnp.einsum("qe,perfj->prfqj", sines, imag_part, precision=high)
    )
    east_imag = 0.5 * (
        jnp.einsum("qe,perfj->prfqj", cosines, imag_part, precision=high)
        - jnp.einsum("qe,perfj->prfqj", sines, real_part, precision=high)
    )
    power = 0.5 * jnp.sum(east_real * east_real + east_imag * east_imag, axis=0)
    return power.reshape(power.shape[0], power.shape[1], -1)


def dedisperse(spectrum, dm_delay, frames):
    base_cos, base_sin = phase_pair(jnp.transpose(dm_delay), frames)
    beams_dev = spectrum.shape[3]
    nfreq = spectrum.shape[2]

    def one_term(carry, block):
        cosine, sine = carry
        cos_half = cosine.astype(jnp.bfloat16)
        sin_half = sine.astype(jnp.bfloat16)
        upper = jnp.concatenate([cos_half, sin_half], axis=1)
        lower = jnp.concatenate([-sin_half, cos_half], axis=1)
        right = jnp.concatenate([upper, lower], axis=0)
        left = block.reshape(2 * nfreq, beams_dev)
        result = lax.dot_general(
            left, right, (((0,), (0,)), ((), ())), preferred_element_type=jnp.float32
        )
        next_cos = cosine * base_cos - sine * base_sin
        next_sin = sine * base_cos + cosine * base_sin
        return ((next_cos, next_sin), result)

    start = (jnp.ones(base_cos.shape, jnp.float32), jnp.zeros(base_cos.shape, jnp.float32))
    _, trials = lax.scan(one_term, start, spectrum)
    return trials.reshape(trials.shape[0], beams_dev, 2, -1)


def synthesis(trials, frames, nfreq):
    terms = frames // 2 + 1
    moment = lax.broadcasted_iota(jnp.int32, (frames, terms), 0)
    harmonic = lax.broadcasted_iota(jnp.int32, (frames, terms), 1)
    cosine, sine = phase_pair(moment * harmonic, frames)
    weight = jnp.where((harmonic == 0) | (harmonic * 2 == frames), 1.0, 2.0).astype(jnp.float32)
    weight = weight / (frames * math.sqrt(nfreq))
    table = jnp.stack([cosine * weight, -sine * weight], axis=1)
    return jnp.einsum("tuk,kbud->btd", table, trials, precision=lax.Precision.HIGHEST)


def plain_body(raw, cell_feed, dm_delay):
    feed_dev, frames, samples = raw.shape
    nfreq = samples // 2
    table = channel_table(samples, nfreq)
    spectra = jnp.dot(
        raw.reshape(feed_dev * frames, samples), table, preferred_element_type=jnp.float32
    )
    spectra = spectra.astype(jnp.bfloat16).reshape(feed_dev, frames, 2, nfreq)
    cells = cell_feed.shape[0] // 4
    polar = lax.broadcasted_iota(jnp.int32, (2, 4, cells), 0)
    feed_index = 2 * cell_feed.reshape(1, 4, cells) + polar
    table_sky = sky_table(cells)
    arrived = lax.all_to_all(spectra, "wide", split_axis=3, concat_axis=0, tiled=True)
    power = beam_power(arrived, feed_index, table_sky)
    centred = (power - jnp.mean(power, axis=0, keepdims=True)).astype(jnp.bfloat16)
    time_table = transform_table(frames)
    local = jnp.einsum("okr,rfb->kofb", time_table, centred, preferred_element_type=jnp.float32)
    spectrum = lax.all_to_all(
        local.astype(jnp.bfloat16), "wide", split_axis=3, concat_axis=2, tiled=True
    )
    trials = dedisperse(spectrum, dm_delay, frames)
    return synthesis(trials, frames, nfreq)


def params(steps=1):
    return pltpu.CompilerParams(
        dimension_semantics=("arbitrary",) * steps, vmem_limit_bytes=VMEM_LIMIT
    )


def cost(flops, nbytes):
    return pl.CostEstimate(flops=int(flops), bytes_accessed=int(nbytes), transcendentals=0)


def angle_tables(samples, parts, kdev, low):
    freq = np.arange(parts)[:, None] * kdev + np.tile(np.arange(kdev), 2)[None, :]
    quarter = np.repeat(np.arange(2), kdev) * (samples // 4)
    coarse = np.arange(0, samples, low)[None, :, None] * freq[:, None, :] % samples
    fine = (np.arange(low)[None, :, None] * freq[:, None, :] + quarter) % samples
    turn = 2.0 * np.pi / samples
    factor = 1.0 / math.sqrt(samples)
    first = np.stack([np.cos(coarse * turn), np.sin(coarse * turn)])
    second = np.stack([np.cos(fine * turn), np.sin(fine * turn)]) * factor
    return first.astype(np.float32), second.astype(np.float32)


def channelise_kernel(low, begin, frames, me_ref, coarse_ref, fine_ref, raw_ref, *refs):
    split = len(refs) > 4
    out_refs = refs[:-4] if split else refs[:1]
    table, rows, order = refs[-4:-1] if split else refs[1:]
    out_ref = refs[-1] if split else refs[0]
    _, samples, _ = table.shape
    parts, count, pols, antennas, lanes = out_ref.shape
    own = order.shape[0]
    steps = rows.shape[0] // own
    group = antennas // steps
    pairs = parts // 2
    step = pl.program_id(0)

    def make(pair, slot):
        for side in range(2):
            part = 2 * pair + side
            fine_cos, fine_sin = fine_ref[0, part], fine_ref[1, part]
            for block in range(samples // low):
                cos_a = coarse_ref[0, part, block : block + 1, :]
                sin_a = coarse_ref[1, part, block : block + 1, :]
                value = cos_a * fine_cos - sin_a * fine_sin
                table[slot, block * low : (block + 1) * low, side * lanes : (side + 1) * lanes] = (
                    value.astype(jnp.bfloat16)
                )

    @pl.when(step == 0)
    def _():
        line = lax.broadcasted_iota(jnp.int32, order.shape, 0)
        column = lax.broadcasted_iota(jnp.int32, order.shape, 1)
        bits, pol_bits = group.bit_length() - 1, pols.bit_length() - 1
        antenna, pol = line & (group - 1), (line >> bits) & (pols - 1)
        wanted = (antenna * pols + pol) * frames + begin + (line >> (bits + pol_bits))
        order[...] = jnp.where(wanted == column, 1.0, 0.0).astype(jnp.bfloat16)
        make(0, 0)

    source = raw_ref[...].reshape(-1, samples)
    ordered = jnp.dot(order[...], source, preferred_element_type=jnp.float32)
    rows[pl.ds(pl.multiple_of(step * own, own), own), :] = ordered.astype(jnp.bfloat16)

    def use(pair, slot):
        value = jnp.dot(rows[...], table[slot], preferred_element_type=jnp.float32)
        value = value.astype(jnp.bfloat16)
        for side in range(2):
            for i in range(steps):
                block = value[i * own : (i + 1) * own, side * lanes : (side + 1) * lanes]
                out_ref[2 * pair + side, :, :, i * group : (i + 1) * group, :] = block.reshape(
                    count, pols, group, lanes
                )

    @pl.when(step == steps - 1)
    def _():
        def one(twice, carry):
            for slot in range(2):
                pair = 2 * twice + slot
                make(lax.rem(pair + 1, pairs), 1 - slot)
                use(pair, slot)
            return carry

        lax.fori_loop(0, pairs // 2, one, 0)
        if split:
            for part in range(parts):
                out_refs[part][...] = out_ref[lax.rem(me_ref[0] + part, parts)]


def channelise(raw, me, first, count, parts, split):
    feed_dev, frames, samples = raw.shape
    kdev = samples // 2 // parts
    low = 64
    group = 16
    steps = feed_dev // (2 * group)
    coarse, fine = angle_tables(samples, parts, kdev, low)
    own = 2 * group * count
    piece = (count, 2, feed_dev // 2, LANES)
    shapes = [piece] * parts if split else [(parts, *piece)]
    whole = lambda shape: pl.BlockSpec(shape, lambda i, me_ref: (0,) * len(shape))
    scratch = [
        pltpu.VMEM((2, samples, 2 * LANES), jnp.bfloat16),
        pltpu.VMEM((steps * own, samples), jnp.bfloat16),
        pltpu.VMEM((own, 2 * group * frames), jnp.bfloat16),
    ]
    if split:
        scratch.append(pltpu.VMEM((parts, *piece), jnp.bfloat16))
    result = pl.pallas_call(
        functools.partial(channelise_kernel, low, first, frames),
        name="channelise",
        grid_spec=pltpu.PrefetchScalarGridSpec(
            num_scalar_prefetch=1,
            grid=(steps,),
            in_specs=[
                whole(coarse.shape),
                whole(fine.shape),
                pl.BlockSpec((2 * group, frames, samples), lambda i, me_ref: (i, 0, 0)),
            ],
            out_specs=[whole(shape) for shape in shapes],
            scratch_shapes=scratch,
        ),
        out_shape=[jax.ShapeDtypeStruct(shape, jnp.bfloat16) for shape in shapes],
        compiler_params=params(),
        cost_estimate=cost(
            2 * feed_dev * count * samples * samples, 4 * raw.size
        ),
    )(me, jnp.asarray(coarse), jnp.asarray(fine), raw)
    return result if split else result[0]


def beam_table(cell_feed, me, parts):
    beams = cell_feed.shape[0]
    cells = beams // 4
    own = beams // parts
    antenna = lax.broadcasted_iota(jnp.int32, (beams, beams), 0)
    cell = lax.broadcasted_iota(jnp.int32, (beams, beams), 1)
    antenna = (me - antenna // own + parts) % parts * own + antenna % own
    place = jnp.sum(jnp.where(cell_feed[None, :] == antenna, cell, 0), axis=1)
    east, north = place // cells, place % cells
    count = lax.broadcasted_iota(jnp.int32, (cells, beams), 0) * north[None, :]
    cosine, sine = phase_pair(count, cells)
    factor = 1.0 / math.sqrt(cells)
    cosine = (cosine * factor).astype(jnp.bfloat16)
    sine = (sine * factor).astype(jnp.bfloat16)
    cosine, sine = lax.optimization_barrier((cosine, sine))
    quarters = jnp.arange(4, dtype=jnp.int32)[:, None, None] * east % 4
    odd, minus = quarters % 2 == 1, quarters >= 2
    real = jnp.where(odd, -sine, cosine)
    imag = jnp.where(odd, -cosine, -sine)
    table = jnp.stack([jnp.where(minus, -real, real), jnp.where(minus, -imag, imag)])
    order = (me + jnp.arange(parts, dtype=jnp.int32)) % parts
    return jnp.take(table.reshape(2, parts, own, beams), order, axis=1).reshape(2, beams, beams)


def beam_kernel(frames, n_spec, n_prev, me_ref, weight_ref, *refs):
    spec_refs, prev_refs = refs[:n_spec], refs[n_spec : n_spec + n_prev]
    out_refs, right = refs[n_spec + n_prev : -1], refs[-1]
    last = len(out_refs) > 1
    count, pols, group, lanes = spec_refs[0].shape[-4:]
    tile = weight_ref.shape[1]
    parts = weight_ref.shape[2] // group
    half = lanes // 2
    pairs = count // 2

    @pl.when(pl.program_id(0) == 0)
    def _():
        for d in range(parts):
            for r in range(count):
                for p in range(pols):
                    at = (r % 2 * pols + p) * lanes
                    if n_spec == 1:
                        block = spec_refs[0][lax.rem(me_ref[0] + (parts - d), parts), r, p]
                    else:
                        block = spec_refs[d][r, p]
                    right[r // 2, d * group : (d + 1) * group, at : at + lanes] = block

    low = lax.broadcasted_iota(jnp.int32, (tile, lanes), 1) < half
    sign = jnp.where(low, -1.0, 1.0)

    def power_of(pair):
        first = jnp.dot(weight_ref[0], right[pair], preferred_element_type=jnp.float32)
        second = jnp.dot(weight_ref[1], right[pair], preferred_element_type=jnp.float32)
        sums = []
        for r in range(2):
            total = None
            for p in range(pols):
                cut = slice((r * pols + p) * lanes, (r * pols + p + 1) * lanes)
                turned = pltpu.roll(second[:, cut], half, 1)
                value = first[:, cut] + sign * turned
                total = value * value if total is None else total + value * value
            sums.append(0.125 * (total + pltpu.roll(total, half, 1)))
        return jnp.where(low, sums[0], sums[1])

    if not last:

        def one(pair, carry):
            out_refs[0][pair] = power_of(pair)
            return carry

        lax.fori_loop(0, pairs, one, 0)

    if last:
        powers = [power_of(pair) for pair in range(pairs)]
        blocks = [ref[i] for ref in prev_refs for i in range(ref.shape[0])] + powers
        total = functools.reduce(lambda a, b: a + b, blocks)
        mean = (total + pltpu.roll(total, half, 1)) * (1.0 / frames)
        hold = out_refs[-1]
        own = hold.shape[2]
        per = tile // own
        at = pl.program_id(0) * per
        for i, block in enumerate(blocks):
            hold[pl.ds(at, per), i] = (block - mean).astype(jnp.bfloat16).reshape(per, own, lanes)

        @pl.when(pl.program_id(0) == pl.num_programs(0) - 1)
        def _():
            for part in range(hold.shape[0]):
                out_refs[part][...] = hold[part]


def beam_stage(weights, me, arrived, frames, parts, prev=None, share=(0, 1)):
    count, pols, group, lanes = arrived[0].shape[-4:]
    beams = weights.shape[1]
    tile = 256
    whole = lambda shape: pl.BlockSpec(shape, lambda i, me_ref: (0,) * len(shape))
    steps = beams // tile // share[1]
    begin = steps * share[0]
    rows = lambda power: pl.BlockSpec(
        (power.shape[0], tile, lanes), lambda i, me_ref: (0, begin + i, 0)
    )
    scratch = [pltpu.VMEM((count // 2, parts * group, 2 * pols * lanes), jnp.bfloat16)]
    before = prev or []
    if prev is None:
        out_shape = [jax.ShapeDtypeStruct((count // 2, beams, lanes), jnp.float32)]
        out_specs = [rows(out_shape[0])]
    else:
        piece = (frames // 2, beams // parts, lanes)
        out_shape = [jax.ShapeDtypeStruct(piece, jnp.bfloat16)] * (parts // share[1])
        out_specs = [whole(piece)] * (parts // share[1])
        scratch.insert(0, pltpu.VMEM((parts // share[1], *piece), jnp.bfloat16))
    result = pl.pallas_call(
        functools.partial(beam_kernel, frames, len(arrived), len(before)),
        name="beams",
        grid_spec=pltpu.PrefetchScalarGridSpec(
            num_scalar_prefetch=1,
            grid=(steps,),
            in_specs=[pl.BlockSpec((2, tile, beams), lambda i, me_ref: (0, begin + i, 0))]
            + [whole(piece.shape) for piece in arrived]
            + [rows(power) for power in before],
            out_specs=out_specs,
            scratch_shapes=scratch,
        ),
        out_shape=out_shape,
        compiler_params=params(),
        cost_estimate=cost(
            4 * beams * beams * count * pols * lanes // share[1],
            4 * weights.size + 4 * beams * count * lanes,
        ),
    )(me, weights, *arrived, *before)
    return result[0] if prev is None else result


def turn_value(count, frames):
    folded = jnp.minimum(count, frames - count)
    inner = jnp.minimum(folded, frames // 2 - folded)
    value = jnp.zeros(count.shape, jnp.float32)
    for i in range(frames // 4):
        value = jnp.where(inner == i, np.float32(math.cos(2.0 * math.pi * i / frames)), value)
    return jnp.where(folded > frames // 4, -value, value)


def factor_kernel(frames, delay_ref, out_ref):
    delay = delay_ref[...]
    quarter = frames // 4
    for h in range(1, quarter + 1):
        count = (h * delay) & (frames - 1)
        shifted = (count + (frames - quarter)) & (frames - 1)
        out_ref[2 * h - 2] = turn_value(count, frames).astype(jnp.bfloat16)
        out_ref[2 * h - 1] = turn_value(shifted, frames).astype(jnp.bfloat16)
    out_ref[2 * quarter] = jnp.where((delay & 1) == 1, -1.0, 1.0).astype(jnp.bfloat16)


def factor_stage(delay, frames):
    nfreq, trials = delay.shape
    rows = 32
    terms = frames // 2 + 1
    return pl.pallas_call(
        functools.partial(factor_kernel, frames),
        name="factors",
        grid=(nfreq // rows,),
        in_specs=[pl.BlockSpec((rows, trials), lambda i: (i, 0))],
        out_specs=pl.BlockSpec((terms, rows, trials), lambda i: (0, i, 0)),
        out_shape=jax.ShapeDtypeStruct((terms, nfreq, trials), jnp.bfloat16),
        compiler_params=params(),
        cost_estimate=cost(10 * terms * nfreq * trials, 2 * terms * nfreq * trials),
    )(delay)


def rounded(value):
    return float(np.asarray(value, np.float32).astype(jnp.bfloat16).astype(np.float32))


def turns(count, frames):
    angle = 2.0 * math.pi * (count % frames) / frames
    pair = []
    for value in (math.cos(angle), math.sin(angle)):
        pair.append(float(round(value)) if abs(value - round(value)) < 1e-12 else value)
    return pair


def weighted(terms):
    total = None
    for factor, value in terms:
        if factor == 0.0:
            continue
        term = value if factor == 1.0 else (-value if factor == -1.0 else factor * value)
        total = term if total is None else total + term
    return total


def harmonics_of(values, frames):
    half, quarter = frames // 2, frames // 4
    plus = [values[r] + values[r + half] for r in range(half)]
    minus = [values[r] - values[r + half] for r in range(half)]
    result = []
    for h in range(half + 1):
        base = minus if h % 2 else plus
        real, imag = [(1.0, base[0])], []
        for r in range(1, quarter):
            cosine, sine = (rounded(x) for x in turns(h * r, frames))
            other = base[half - r]
            even = base[r] - other if h % 2 else base[r] + other
            odd = base[r] + other if h % 2 else base[r] - other
            real.append((cosine, even))
            imag.append((-sine, odd))
        cosine, sine = (rounded(x) for x in turns(h * quarter, frames))
        real.append((cosine, base[quarter]))
        imag.append((-sine, base[quarter]))
        result.append((weighted(real), weighted(imag)))
    return result


def dedisperse_kernel(frames, nfreq, me_ref, *refs):
    arrived_refs, (factors_ref, out_ref, held, left, zero, slots, sems) = refs[:-7], refs[-7:]
    parts = len(arrived_refs)
    pairs, own, lanes = arrived_refs[0].shape
    half, quarter = frames // 2, frames // 4
    step, steps = pl.program_id(0), pl.num_programs(0)
    tile = slots.shape[3]

    def fetch(at, slot):
        cut = pl.ds(pl.multiple_of(at * tile, tile), tile)
        return pltpu.make_async_copy(factors_ref.at[:, :, cut], slots.at[slot], sems.at[slot])

    @pl.when(step == 0)
    def _():
        fetch(0, 0).start()
        low = lax.broadcasted_iota(jnp.int32, (own, lanes), 1) < lanes // 2
        zero[...] = jnp.zeros_like(zero)
        for d in range(parts):
            held[lax.rem(me_ref[0] + (parts - d), parts)] = arrived_refs[d][...]

        def one(j, carry):
            values = []
            for i in range(pairs):
                even = held[2 * j, i].astype(jnp.float32)
                odd = held[2 * j + 1, i].astype(jnp.float32)
                values.append(jnp.where(low, even, pltpu.roll(odd, lanes // 2, 1)))
                values.append(jnp.where(low, pltpu.roll(even, lanes // 2, 1), odd))
            terms = harmonics_of(values, frames)
            zero[...] += terms[0][0].astype(jnp.bfloat16).astype(jnp.float32)
            for h in range(1, half + 1):
                left[j, h - 1, :own, :] = terms[h][0].astype(jnp.bfloat16)
                if h < half:
                    left[j, h - 1, own:, :] = terms[h][1].astype(jnp.bfloat16)
            return carry

        lax.fori_loop(0, parts // 2, one, 0)

    slot = lax.rem(step, 2)

    @pl.when(step + 1 < steps)
    def _():
        fetch(step + 1, 1 - slot).start()

    fetch(step, slot).wait()
    factor_ref = slots.at[slot]
    scale = 1.0 / (frames * math.sqrt(nfreq))
    first = scale * jnp.sum(zero[...], axis=1, keepdims=True)
    real, imag = [], []
    parity = factor_ref[2 * quarter]
    for h in range(1, half):
        block = jnp.concatenate([left[j, h - 1] for j in range(parts // 2)], axis=1)
        base = min(h, half - h)
        cosines, sines = factor_ref[2 * base - 2], factor_ref[2 * base - 1]
        if h > quarter:
            cosines, sines = cosines * parity, sines * -parity
        by_cos = jnp.dot(block, cosines, preferred_element_type=jnp.float32)
        by_sin = jnp.dot(block, sines, preferred_element_type=jnp.float32)
        real.append((2.0 * scale) * (by_cos[:own] - by_sin[own:]))
        imag.append((2.0 * scale) * (by_sin[:own] + by_cos[own:]))
    block = jnp.concatenate([left[j, half - 1, :own, :] for j in range(parts // 2)], axis=1)
    last = scale * jnp.dot(block, parity, preferred_element_type=jnp.float32)
    for t in range(half):
        sums = []
        for odd in range(2):
            terms = []
            for h in range(2 - odd, half, 2):
                cosine, sine = turns(h * t, frames)
                terms.append((cosine, real[h - 1]))
                terms.append((-sine, imag[h - 1]))
            sums.append(weighted(terms))
        even = sums[0] + first + (last if t % 2 == 0 else -last)
        out_ref[:, t, :] = even + sums[1]
        out_ref[:, t + half, :] = even - sums[1]


def dedisperse_stage(me, arrived, factors, frames):
    pairs, own, lanes = arrived[0].shape
    parts = len(arrived)
    terms, nfreq, trials = factors.shape
    tile = 2 * LANES
    whole = lambda shape: pl.BlockSpec(shape, lambda i, me_ref: (0,) * len(shape))
    return pl.pallas_call(
        functools.partial(dedisperse_kernel, frames, nfreq),
        name="dedisperse",
        grid_spec=pltpu.PrefetchScalarGridSpec(
            num_scalar_prefetch=1,
            grid=(trials // tile,),
            in_specs=[whole(piece.shape) for piece in arrived]
            + [pl.BlockSpec(memory_space=pl.ANY)],
            out_specs=pl.BlockSpec((own, frames, tile), lambda i, me_ref: (0, 0, i)),
            scratch_shapes=[
                pltpu.VMEM((parts, pairs, own, lanes), jnp.bfloat16),
                pltpu.VMEM((parts // 2, frames // 2, 2 * own, lanes), jnp.bfloat16),
                pltpu.VMEM((own, lanes), jnp.float32),
                pltpu.VMEM((2, terms, nfreq, tile), jnp.bfloat16),
                pltpu.SemaphoreType.DMA((2,)),
            ],
        ),
        out_shape=jax.ShapeDtypeStruct((own, frames, trials), jnp.float32),
        compiler_params=params(),
        cost_estimate=cost(
            8 * own * terms * nfreq * trials, 2 * factors.size + 4 * own * frames * trials
        ),
    )(me, *arrived, factors)


def chunks_of(frames):
    end = max(2, frames // 4)
    return ((0, end, False), (end, frames - 2 * end, True), (frames - end, end, False))


def shifted(piece, by, parts):
    return lax.ppermute(piece, "wide", [(i, (i + by) % parts) for i in range(parts)])


def exchange(message, parts):
    if not isinstance(message, (list, tuple)):
        return [lax.all_to_all(message, "wide", split_axis=0, concat_axis=0, tiled=True)]
    return [message[0]] + [shifted(message[d], d, parts) for d in range(1, parts)]


def tiled_body(parts, raw, cell_feed, dm_delay):
    _, frames, _ = raw.shape
    me = lax.axis_index("wide").astype(jnp.int32)
    own = me.reshape(1)
    cuts = chunks_of(frames)
    messages = []
    for first, count, split in cuts:
        message = channelise(raw, own, first, count, parts, split)
        raw, cell_feed, dm_delay, message = lax.optimization_barrier(
            (raw, cell_feed, dm_delay, message)
        )
        messages.append(message)
    weights = beam_table(cell_feed, me, parts)
    factors = factor_stage(jnp.transpose(dm_delay), frames)
    messages[-1], factors = lax.optimization_barrier((messages[-1], factors))
    powers = []
    for message in messages[:-1]:
        power = beam_stage(weights, own, exchange(message, parts), frames, parts)
        weights, power = lax.optimization_barrier((weights, power))
        powers.append(power)
    tail = exchange(messages[-1], parts)
    early = beam_stage(weights, own, tail, frames, parts, powers, (0, 2))
    half = len(early)
    arrived = [early[0]] + [shifted(early[d], d, parts) for d in range(1, half)]
    weights, arrived[0] = lax.optimization_barrier((weights, arrived[0]))
    late = beam_stage(weights, own, tail, frames, parts, powers, (1, 2))
    arrived += [shifted(late[d], half + d, parts) for d in range(half)]
    return dedisperse_stage(own, arrived, factors, frames)


def fits(parts, raw_shape, cells, delay_shape):
    feed_dev, frames, samples = raw_shape
    trials, nfreq = delay_shape
    return (
        samples // parts == LANES
        and nfreq * 2 == samples
        and samples % (2 * LANES) == 0
        and feed_dev % 32 == 0
        and frames % 16 == 0
        and frames & (frames - 1) == 0
        and cells % 512 == 0
        and cells // parts == LANES // 2
        and trials % (2 * LANES) == 0
        and parts % 4 == 0
    )


def solution(mesh):
    parts = mesh.shape["wide"]

    def body(raw, cell_feed, dm_delay):
        if fits(parts, raw.shape, cell_feed.shape[0], dm_delay.shape):
            return tiled_body(parts, raw, cell_feed, dm_delay)
        return plain_body(raw, cell_feed, dm_delay)

    placed = (P(("grp", "wide"), None, None), P(), P())
    return jax.shard_map(
        body, mesh=mesh, in_specs=placed, out_specs=P(("grp", "wide"), None, None), check_vma=False
    )
```

```python
import functools
import math

import jax
import jax.numpy as jnp
import numpy as np
from jax import lax
from jax.experimental import pallas as pl
from jax.experimental.pallas import tpu as pltpu
from jax.sharding import PartitionSpec as P


LANES = 128
VMEM_LIMIT = 58 * 1024 * 1024

EAST_COSINE = np.array([[1, 1, 1, 1], [1, 0, -1, 0], [1, -1, 1, -1], [1, 0, -1, 0]], np.float32)
EAST_SINE = np.array([[0, 0, 0, 0], [0, 1, 0, -1], [0, 0, 0, 0], [0, -1, 0, 1]], np.float32)


def phase_pair(count, length):
    angle = (count % length).astype(jnp.float32) * (2.0 * math.pi / length)
    return (jnp.cos(angle), jnp.sin(angle))


def channel_table(samples, width):
    sample_ids = lax.broadcasted_iota(jnp.int32, (samples, width), 0)
    freq_ids = lax.broadcasted_iota(jnp.int32, (samples, width), 1)
    cosine, sine = phase_pair(sample_ids * freq_ids, samples)
    factor = 1.0 / math.sqrt(samples)
    return jnp.concatenate([cosine * factor, -sine * factor], axis=1).astype(jnp.bfloat16)


def sky_table(cells):
    rows = lax.broadcasted_iota(jnp.int32, (cells, cells), 0)
    cols = lax.broadcasted_iota(jnp.int32, (cells, cells), 1)
    cosine, sine = phase_pair(rows * cols, cells)
    real_row = jnp.stack([cosine, sine], axis=-1)
    imag_row = jnp.stack([-sine, cosine], axis=-1)
    factor = 1.0 / math.sqrt(cells)
    return (jnp.stack([real_row, imag_row], axis=1) * factor).astype(jnp.bfloat16)


def transform_table(frames):
    terms = frames // 2 + 1
    harmonic = lax.broadcasted_iota(jnp.int32, (terms, frames), 0)
    moment = lax.broadcasted_iota(jnp.int32, (terms, frames), 1)
    cosine, sine = phase_pair(harmonic * moment, frames)
    return jnp.stack([cosine, -sine]).astype(jnp.bfloat16)


def beam_power(spec, feed_index, table):
    grid = jnp.take(spec, feed_index.reshape(-1), axis=0)
    grid = grid.reshape(feed_index.shape + spec.shape[1:])
    beams = jnp.einsum("joni,penrif->poerfj", table, grid, preferred_element_type=jnp.float32)
    real_part = beams[:, 0]
    imag_part = beams[:, 1]
    cosines = jnp.asarray(EAST_COSINE)
    sines = jnp.asarray(EAST_SINE)
    high = lax.Precision.HIGHEST
    east_real = 0.5 * (
        jnp.einsum("qe,perfj->prfqj", cosines, real_part, precision=high)
        + jnp.einsum("qe,perfj->prfqj", sines, imag_part, precision=high)
    )
    east_imag = 0.5 * (
        jnp.einsum("qe,perfj->prfqj", cosines, imag_part, precision=high)
        - jnp.einsum("qe,perfj->prfqj", sines, real_part, precision=high)
    )
    power = 0.5 * jnp.sum(east_real * east_real + east_imag * east_imag, axis=0)
    return power.reshape(power.shape[0], power.shape[1], -1)


def dedisperse(spectrum, dm_delay, frames):
    base_cos, base_sin = phase_pair(jnp.transpose(dm_delay), frames)
    beams_dev = spectrum.shape[3]
    nfreq = spectrum.shape[2]

    def one_term(carry, block):
        cosine, sine = carry
        cos_half = cosine.astype(jnp.bfloat16)
        sin_half = sine.astype(jnp.bfloat16)
        upper = jnp.concatenate([cos_half, sin_half], axis=1)
        lower = jnp.concatenate([-sin_half, cos_half], axis=1)
        right = jnp.concatenate([upper, lower], axis=0)
        left = block.reshape(2 * nfreq, beams_dev)
        result = lax.dot_general(
            left, right, (((0,), (0,)), ((), ())), preferred_element_type=jnp.float32
        )
        next_cos = cosine * base_cos - sine * base_sin
        next_sin = sine * base_cos + cosine * base_sin
        return ((next_cos, next_sin), result)

    start = (jnp.ones(base_cos.shape, jnp.float32), jnp.zeros(base_cos.shape, jnp.float32))
    _, trials = lax.scan(one_term, start, spectrum)
    return trials.reshape(trials.shape[0], beams_dev, 2, -1)


def synthesis(trials, frames, nfreq):
    terms = frames // 2 + 1
    moment = lax.broadcasted_iota(jnp.int32, (frames, terms), 0)
    harmonic = lax.broadcasted_iota(jnp.int32, (frames, terms), 1)
    cosine, sine = phase_pair(moment * harmonic, frames)
    weight = jnp.where((harmonic == 0) | (harmonic * 2 == frames), 1.0, 2.0).astype(jnp.float32)
    weight = weight / (frames * math.sqrt(nfreq))
    table = jnp.stack([cosine * weight, -sine * weight], axis=1)
    return jnp.einsum("tuk,kbud->btd", table, trials, precision=lax.Precision.HIGHEST)


def plain_body(raw, cell_feed, dm_delay):
    feed_dev, frames, samples = raw.shape
    nfreq = samples // 2
    table = channel_table(samples, nfreq)
    spectra = jnp.dot(
        raw.reshape(feed_dev * frames, samples), table, preferred_element_type=jnp.float32
    )
    spectra = spectra.astype(jnp.bfloat16).reshape(feed_dev, frames, 2, nfreq)
    cells = cell_feed.shape[0] // 4
    polar = lax.broadcasted_iota(jnp.int32, (2, 4, cells), 0)
    feed_index = 2 * cell_feed.reshape(1, 4, cells) + polar
    table_sky = sky_table(cells)
    arrived = lax.all_to_all(spectra, "wide", split_axis=3, concat_axis=0, tiled=True)
    power = beam_power(arrived, feed_index, table_sky)
    centred = (power - jnp.mean(power, axis=0, keepdims=True)).astype(jnp.bfloat16)
    time_table = transform_table(frames)
    local = jnp.einsum("okr,rfb->kofb", time_table, centred, preferred_element_type=jnp.float32)
    spectrum = lax.all_to_all(
        local.astype(jnp.bfloat16), "wide", split_axis=3, concat_axis=2, tiled=True
    )
    trials = dedisperse(spectrum, dm_delay, frames)
    return synthesis(trials, frames, nfreq)


def params(steps=1):
    return pltpu.CompilerParams(
        dimension_semantics=("arbitrary",) * steps, vmem_limit_bytes=VMEM_LIMIT
    )


def cost(flops, nbytes):
    return pl.CostEstimate(flops=int(flops), bytes_accessed=int(nbytes), transcendentals=0)


def angle_tables(samples, parts, kdev, low):
    freq = np.arange(parts)[:, None] * kdev + np.tile(np.arange(kdev), 2)[None, :]
    quarter = np.repeat(np.arange(2), kdev) * (samples // 4)
    coarse = np.arange(0, samples, low)[None, :, None] * freq[:, None, :] % samples
    fine = (np.arange(low)[None, :, None] * freq[:, None, :] + quarter) % samples
    turn = 2.0 * np.pi / samples
    factor = 1.0 / math.sqrt(samples)
    first = np.stack([np.cos(coarse * turn), np.sin(coarse * turn)])
    second = np.stack([np.cos(fine * turn), np.sin(fine * turn)]) * factor
    return first.astype(np.float32), second.astype(np.float32)


def channelise_kernel(low, begin, frames, me_ref, coarse_ref, fine_ref, raw_ref, *refs):
    split = len(refs) > 4
    out_refs = refs[:-4] if split else refs[:1]
    table, rows, order = refs[-4:-1] if split else refs[1:]
    out_ref = refs[-1] if split else refs[0]
    _, samples, _ = table.shape
    parts, count, pols, antennas, lanes = out_ref.shape
    own = order.shape[0]
    steps = rows.shape[0] // own
    group = antennas // steps
    pairs = parts // 2
    step = pl.program_id(0)

    def make(pair, slot):
        for side in range(2):
            part = 2 * pair + side
            fine_cos, fine_sin = fine_ref[0, part], fine_ref[1, part]
            for block in range(samples // low):
                cos_a = coarse_ref[0, part, block : block + 1, :]
                sin_a = coarse_ref[1, part, block : block + 1, :]
                value = cos_a * fine_cos - sin_a * fine_sin
                table[slot, block * low : (block + 1) * low, side * lanes : (side + 1) * lanes] = (
                    value.astype(jnp.bfloat16)
                )

    @pl.when(step == 0)
    def _():
        line = lax.broadcasted_iota(jnp.int32, order.shape, 0)
        column = lax.broadcasted_iota(jnp.int32, order.shape, 1)
        bits, pol_bits = group.bit_length() - 1, pols.bit_length() - 1
        antenna, pol = line & (group - 1), (line >> bits) & (pols - 1)
        wanted = (antenna * pols + pol) * frames + begin + (line >> (bits + pol_bits))
        order[...] = jnp.where(wanted == column, 1.0, 0.0).astype(jnp.bfloat16)
        make(0, 0)

    source = raw_ref[...].reshape(-1, samples)
    ordered = jnp.dot(order[...], source, preferred_element_type=jnp.float32)
    rows[pl.ds(pl.multiple_of(step * own, own), own), :] = ordered.astype(jnp.bfloat16)

    def use(pair, slot):
        value = jnp.dot(rows[...], table[slot], preferred_element_type=jnp.float32)
        value = value.astype(jnp.bfloat16)
        for side in range(2):
            for i in range(steps):
                block = value[i * own : (i + 1) * own, side * lanes : (side + 1) * lanes]
                out_ref[2 * pair + side, :, :, i * group : (i + 1) * group, :] = block.reshape(
                    count, pols, group, lanes
                )

    @pl.when(step == steps - 1)
    def _():
        def one(twice, carry):
            for slot in range(2):
                pair = 2 * twice + slot
                make(lax.rem(pair + 1, pairs), 1 - slot)
                use(pair, slot)
            return carry

        lax.fori_loop(0, pairs // 2, one, 0)
        if split:
            for part in range(parts):
                out_refs[part][...] = out_ref[lax.rem(me_ref[0] + part, parts)]


def channelise(raw, me, first, count, parts, split):
    feed_dev, frames, samples = raw.shape
    kdev = samples // 2 // parts
    low = 64
    group = 16
    steps = feed_dev // (2 * group)
    coarse, fine = angle_tables(samples, parts, kdev, low)
    own = 2 * group * count
    piece = (count, 2, feed_dev // 2, LANES)
    shapes = [piece] * parts if split else [(parts, *piece)]
    whole = lambda shape: pl.BlockSpec(shape, lambda i, me_ref: (0,) * len(shape))
    scratch = [
        pltpu.VMEM((2, samples, 2 * LANES), jnp.bfloat16),
        pltpu.VMEM((steps * own, samples), jnp.bfloat16),
        pltpu.VMEM((own, 2 * group * frames), jnp.bfloat16),
    ]
    if split:
        scratch.append(pltpu.VMEM((parts, *piece), jnp.bfloat16))
    result = pl.pallas_call(
        functools.partial(channelise_kernel, low, first, frames),
        name="channelise",
        grid_spec=pltpu.PrefetchScalarGridSpec(
            num_scalar_prefetch=1,
            grid=(steps,),
            in_specs=[
                whole(coarse.shape),
                whole(fine.shape),
                pl.BlockSpec((2 * group, frames, samples), lambda i, me_ref: (i, 0, 0)),
            ],
            out_specs=[whole(shape) for shape in shapes],
            scratch_shapes=scratch,
        ),
        out_shape=[jax.ShapeDtypeStruct(shape, jnp.bfloat16) for shape in shapes],
        compiler_params=params(),
        cost_estimate=cost(
            2 * feed_dev * count * samples * samples, 4 * raw.size
        ),
    )(me, jnp.asarray(coarse), jnp.asarray(fine), raw)
    return result if split else result[0]


def beam_table(cell_feed, me, parts):
    beams = cell_feed.shape[0]
    cells = beams // 4
    own = beams // parts
    antenna = lax.broadcasted_iota(jnp.int32, (beams, beams), 0)
    cell = lax.broadcasted_iota(jnp.int32, (beams, beams), 1)
    antenna = (me - antenna // own + parts) % parts * own + antenna % own
    place = jnp.sum(jnp.where(cell_feed[None, :] == antenna, cell, 0), axis=1)
    east, north = place // cells, place % cells
    count = lax.broadcasted_iota(jnp.int32, (cells, beams), 0) * north[None, :]
    cosine, sine = phase_pair(count, cells)
    factor = 1.0 / math.sqrt(cells)
    cosine = (cosine * factor).astype(jnp.bfloat16)
    sine = (sine * factor).astype(jnp.bfloat16)
    cosine, sine = lax.optimization_barrier((cosine, sine))
    quarters = jnp.arange(4, dtype=jnp.int32)[:, None, None] * east % 4
    odd, minus = quarters % 2 == 1, quarters >= 2
    real = jnp.where(odd, -sine, cosine)
    imag = jnp.where(odd, -cosine, -sine)
    table = jnp.stack([jnp.where(minus, -real, real), jnp.where(minus, -imag, imag)])
    order = (me + parts // 4 + jnp.arange(parts, dtype=jnp.int32)) % parts
    return jnp.take(table.reshape(2, parts, own, beams), order, axis=1).reshape(2, beams, beams)


def beam_kernel(frames, n_spec, n_prev, me_ref, weight_ref, *refs):
    spec_refs, prev_refs = refs[:n_spec], refs[n_spec : n_spec + n_prev]
    out_refs, right = refs[n_spec + n_prev : -1], refs[-1]
    last = len(out_refs) > 1
    count, pols, group, lanes = spec_refs[0].shape[-4:]
    tile = weight_ref.shape[1]
    parts = weight_ref.shape[2] // group
    half = lanes // 2
    pairs = count // 2

    @pl.when(pl.program_id(0) == 0)
    def _():
        for d in range(parts):
            for r in range(count):
                for p in range(pols):
                    at = (r % 2 * pols + p) * lanes
                    if n_spec == 1:
                        block = spec_refs[0][lax.rem(me_ref[0] + (parts - d), parts), r, p]
                    else:
                        block = spec_refs[d][r, p]
                    right[r // 2, d * group : (d + 1) * group, at : at + lanes] = block

    low = lax.broadcasted_iota(jnp.int32, (tile, lanes), 1) < half
    sign = jnp.where(low, -1.0, 1.0)

    def power_of(pair):
        first = jnp.dot(weight_ref[0], right[pair], preferred_element_type=jnp.float32)
        second = jnp.dot(weight_ref[1], right[pair], preferred_element_type=jnp.float32)
        sums = []
        for r in range(2):
            total = None
            for p in range(pols):
                cut = slice((r * pols + p) * lanes, (r * pols + p + 1) * lanes)
                turned = pltpu.roll(second[:, cut], half, 1)
                value = first[:, cut] + sign * turned
                total = value * value if total is None else total + value * value
            sums.append(0.125 * (total + pltpu.roll(total, half, 1)))
        return jnp.where(low, sums[0], sums[1])

    if not last:

        def one(pair, carry):
            out_refs[0][pair] = power_of(pair)
            return carry

        lax.fori_loop(0, pairs, one, 0)

    if last:
        powers = [power_of(pair) for pair in range(pairs)]
        blocks = [ref[i] for ref in prev_refs for i in range(ref.shape[0])] + powers
        total = functools.reduce(lambda a, b: a + b, blocks)
        mean = (total + pltpu.roll(total, half, 1)) * (1.0 / frames)
        hold = out_refs[-1]
        own = hold.shape[2]
        per = tile // own
        at = pl.program_id(0) * per
        for i, block in enumerate(blocks):
            hold[pl.ds(at, per), i] = (block - mean).astype(jnp.bfloat16).reshape(per, own, lanes)

        @pl.when(pl.program_id(0) == pl.num_programs(0) - 1)
        def _():
            for part in range(hold.shape[0]):
                out_refs[part][...] = hold[part]


def beam_stage(weights, me, arrived, frames, parts, prev=None, share=(0, 1)):
    count, pols, group, lanes = arrived[0].shape[-4:]
    beams = weights.shape[1]
    tile = 256
    whole = lambda shape: pl.BlockSpec(shape, lambda i, me_ref: (0,) * len(shape))
    steps = beams // tile // share[1]
    begin = steps * share[0]
    rows = lambda power: pl.BlockSpec(
        (power.shape[0], tile, lanes), lambda i, me_ref: (0, begin + i, 0)
    )
    scratch = [pltpu.VMEM((count // 2, parts * group, 2 * pols * lanes), jnp.bfloat16)]
    before = prev or []
    if prev is None:
        out_shape = [jax.ShapeDtypeStruct((count // 2, beams, lanes), jnp.float32)]
        out_specs = [rows(out_shape[0])]
    else:
        piece = (frames // 2, beams // parts, lanes)
        out_shape = [jax.ShapeDtypeStruct(piece, jnp.bfloat16)] * (parts // share[1])
        out_specs = [whole(piece)] * (parts // share[1])
        scratch.insert(0, pltpu.VMEM((parts // share[1], *piece), jnp.bfloat16))
    result = pl.pallas_call(
        functools.partial(beam_kernel, frames, len(arrived), len(before)),
        name="beams",
        grid_spec=pltpu.PrefetchScalarGridSpec(
            num_scalar_prefetch=1,
            grid=(steps,),
            in_specs=[pl.BlockSpec((2, tile, beams), lambda i, me_ref: (0, begin + i, 0))]
            + [whole(piece.shape) for piece in arrived]
            + [rows(power) for power in before],
            out_specs=out_specs,
            scratch_shapes=scratch,
        ),
        out_shape=out_shape,
        compiler_params=params(),
        cost_estimate=cost(
            4 * beams * beams * count * pols * lanes // share[1],
            4 * weights.size + 4 * beams * count * lanes,
        ),
    )(me, weights, *arrived, *before)
    return result[0] if prev is None else result


def turn_value(count, frames):
    folded = jnp.minimum(count, frames - count)
    inner = jnp.minimum(folded, frames // 2 - folded)
    value = jnp.zeros(count.shape, jnp.float32)
    for i in range(frames // 4):
        value = jnp.where(inner == i, np.float32(math.cos(2.0 * math.pi * i / frames)), value)
    return jnp.where(folded > frames // 4, -value, value)


def factor_kernel(frames, delay_ref, out_ref):
    delay = delay_ref[...]
    quarter = frames // 4
    for h in range(1, quarter + 1):
        count = (h * delay) & (frames - 1)
        shifted = (count + (frames - quarter)) & (frames - 1)
        out_ref[2 * h - 2] = turn_value(count, frames).astype(jnp.bfloat16)
        out_ref[2 * h - 1] = turn_value(shifted, frames).astype(jnp.bfloat16)
    out_ref[2 * quarter] = jnp.where((delay & 1) == 1, -1.0, 1.0).astype(jnp.bfloat16)


def factor_stage(delay, frames):
    nfreq, trials = delay.shape
    rows = 32
    terms = frames // 2 + 1
    return pl.pallas_call(
        functools.partial(factor_kernel, frames),
        name="factors",
        grid=(nfreq // rows,),
        in_specs=[pl.BlockSpec((rows, trials), lambda i: (i, 0))],
        out_specs=pl.BlockSpec((terms, rows, trials), lambda i: (0, i, 0)),
        out_shape=jax.ShapeDtypeStruct((terms, nfreq, trials), jnp.bfloat16),
        compiler_params=params(),
        cost_estimate=cost(10 * terms * nfreq * trials, 2 * terms * nfreq * trials),
    )(delay)


def rounded(value):
    return float(np.asarray(value, np.float32).astype(jnp.bfloat16).astype(np.float32))


def turns(count, frames):
    angle = 2.0 * math.pi * (count % frames) / frames
    pair = []
    for value in (math.cos(angle), math.sin(angle)):
        pair.append(float(round(value)) if abs(value - round(value)) < 1e-12 else value)
    return pair


def weighted(terms):
    total = None
    for factor, value in terms:
        if factor == 0.0:
            continue
        term = value if factor == 1.0 else (-value if factor == -1.0 else factor * value)
        total = term if total is None else total + term
    return total


def harmonics_of(values, frames):
    half, quarter = frames // 2, frames // 4
    plus = [values[r] + values[r + half] for r in range(half)]
    minus = [values[r] - values[r + half] for r in range(half)]
    result = []
    for h in range(half + 1):
        base = minus if h % 2 else plus
        real, imag = [(1.0, base[0])], []
        for r in range(1, quarter):
            cosine, sine = (rounded(x) for x in turns(h * r, frames))
            other = base[half - r]
            even = base[r] - other if h % 2 else base[r] + other
            odd = base[r] + other if h % 2 else base[r] - other
            real.append((cosine, even))
            imag.append((-sine, odd))
        cosine, sine = (rounded(x) for x in turns(h * quarter, frames))
        real.append((cosine, base[quarter]))
        imag.append((-sine, base[quarter]))
        result.append((weighted(real), weighted(imag)))
    return result


def dedisperse_kernel(frames, nfreq, me_ref, *refs):
    arrived_refs, (factors_ref, out_ref, held, left, zero, slots, sems) = refs[:-7], refs[-7:]
    parts = len(arrived_refs)
    pairs, own, lanes = arrived_refs[0].shape
    half, quarter = frames // 2, frames // 4
    step, steps = pl.program_id(0), pl.num_programs(0)
    tile = slots.shape[3]

    def fetch(at, slot):
        cut = pl.ds(pl.multiple_of(at * tile, tile), tile)
        return pltpu.make_async_copy(factors_ref.at[:, :, cut], slots.at[slot], sems.at[slot])

    @pl.when(step == 0)
    def _():
        fetch(0, 0).start()
        low = lax.broadcasted_iota(jnp.int32, (own, lanes), 1) < lanes // 2
        zero[...] = jnp.zeros_like(zero)
        for d in range(parts):
            held[lax.rem(me_ref[0] + (parts - d), parts)] = arrived_refs[d][...]

        def one(j, carry):
            values = []
            for i in range(pairs):
                even = held[2 * j, i].astype(jnp.float32)
                odd = held[2 * j + 1, i].astype(jnp.float32)
                values.append(jnp.where(low, even, pltpu.roll(odd, lanes // 2, 1)))
                values.append(jnp.where(low, pltpu.roll(even, lanes // 2, 1), odd))
            terms = harmonics_of(values, frames)
            zero[...] += terms[0][0].astype(jnp.bfloat16).astype(jnp.float32)
            for h in range(1, half + 1):
                left[j, h - 1, :own, :] = terms[h][0].astype(jnp.bfloat16)
                if h < half:
                    left[j, h - 1, own:, :] = terms[h][1].astype(jnp.bfloat16)
            return carry

        lax.fori_loop(0, parts // 2, one, 0)

    slot = lax.rem(step, 2)

    @pl.when(step + 1 < steps)
    def _():
        fetch(step + 1, 1 - slot).start()

    fetch(step, slot).wait()
    factor_ref = slots.at[slot]
    scale = 1.0 / (frames * math.sqrt(nfreq))
    first = scale * jnp.sum(zero[...], axis=1, keepdims=True)
    real, imag = [], []
    parity = factor_ref[2 * quarter]
    for h in range(1, half):
        block = jnp.concatenate([left[j, h - 1] for j in range(parts // 2)], axis=1)
        base = min(h, half - h)
        cosines, sines = factor_ref[2 * base - 2], factor_ref[2 * base - 1]
        if h > quarter:
            cosines, sines = cosines * parity, sines * -parity
        by_cos = jnp.dot(block, cosines, preferred_element_type=jnp.float32)
        by_sin = jnp.dot(block, sines, preferred_element_type=jnp.float32)
        real.append((2.0 * scale) * (by_cos[:own] - by_sin[own:]))
        imag.append((2.0 * scale) * (by_sin[:own] + by_cos[own:]))
    block = jnp.concatenate([left[j, half - 1, :own, :] for j in range(parts // 2)], axis=1)
    last = scale * jnp.dot(block, parity, preferred_element_type=jnp.float32)
    for t in range(half):
        sums = []
        for odd in range(2):
            terms = []
            for h in range(2 - odd, half, 2):
                cosine, sine = turns(h * t, frames)
                terms.append((cosine, real[h - 1]))
                terms.append((-sine, imag[h - 1]))
            sums.append(weighted(terms))
        even = sums[0] + first + (last if t % 2 == 0 else -last)
        out_ref[:, t, :] = even + sums[1]
        out_ref[:, t + half, :] = even - sums[1]


def dedisperse_stage(me, arrived, factors, frames):
    pairs, own, lanes = arrived[0].shape
    parts = len(arrived)
    terms, nfreq, trials = factors.shape
    tile = 2 * LANES
    whole = lambda shape: pl.BlockSpec(shape, lambda i, me_ref: (0,) * len(shape))
    return pl.pallas_call(
        functools.partial(dedisperse_kernel, frames, nfreq),
        name="dedisperse",
        grid_spec=pltpu.PrefetchScalarGridSpec(
            num_scalar_prefetch=1,
            grid=(trials // tile,),
            in_specs=[whole(piece.shape) for piece in arrived]
            + [pl.BlockSpec(memory_space=pl.ANY)],
            out_specs=pl.BlockSpec((own, frames, tile), lambda i, me_ref: (0, 0, i)),
            scratch_shapes=[
                pltpu.VMEM((parts, pairs, own, lanes), jnp.bfloat16),
                pltpu.VMEM((parts // 2, frames // 2, 2 * own, lanes), jnp.bfloat16),
                pltpu.VMEM((own, lanes), jnp.float32),
                pltpu.VMEM((2, terms, nfreq, tile), jnp.bfloat16),
                pltpu.SemaphoreType.DMA((2,)),
            ],
        ),
        out_shape=jax.ShapeDtypeStruct((own, frames, trials), jnp.float32),
        compiler_params=params(),
        cost_estimate=cost(
            8 * own * terms * nfreq * trials, 2 * factors.size + 4 * own * frames * trials
        ),
    )(me, *arrived, factors)


def chunks_of(frames):
    end = max(2, frames // 4)
    return ((0, end, False), (end, frames - 2 * end, True), (frames - end, end, False))


def shifted(piece, by, parts):
    return lax.ppermute(piece, "wide", [(i, (i + by) % parts) for i in range(parts)])


def exchange(message, parts):
    if not isinstance(message, (list, tuple)):
        return [lax.all_to_all(message, "wide", split_axis=0, concat_axis=0, tiled=True)]
    return [message[0]] + [shifted(message[d], d, parts) for d in range(1, parts)]


def tiled_body(parts, raw, cell_feed, dm_delay):
    _, frames, _ = raw.shape
    me = lax.axis_index("wide").astype(jnp.int32)
    own = me.reshape(1)
    cuts = chunks_of(frames)
    messages = []
    for first, count, split in cuts:
        message = channelise(raw, own, first, count, parts, split)
        raw, cell_feed, dm_delay, message = lax.optimization_barrier(
            (raw, cell_feed, dm_delay, message)
        )
        messages.append(message)
    weights = beam_table(cell_feed, me, parts)
    factors = factor_stage(jnp.transpose(dm_delay), frames)
    messages[-1], factors = lax.optimization_barrier((messages[-1], factors))
    powers = []
    for message in messages[:-1]:
        power = beam_stage(weights, own, exchange(message, parts), frames, parts)
        weights, power = lax.optimization_barrier((weights, power))
        powers.append(power)
    tail = exchange(messages[-1], parts)
    early = beam_stage(weights, own, tail, frames, parts, powers, (0, 2))
    half, turn = len(early), parts // 4
    arrived = [None] * parts
    for i, piece in enumerate(early):
        arrived[turn + i] = shifted(piece, turn + i, parts)
    weights, powers[0] = lax.optimization_barrier((weights, powers[0]))
    late = beam_stage(weights, own, tail, frames, parts, powers, (1, 2))
    for i, piece in enumerate(late):
        by = (turn + half + i) % parts
        arrived[by] = shifted(piece, by, parts) if by else piece
    return dedisperse_stage(own, arrived, factors, frames)


def fits(parts, raw_shape, cells, delay_shape):
    feed_dev, frames, samples = raw_shape
    trials, nfreq = delay_shape
    return (
        samples // parts == LANES
        and nfreq * 2 == samples
        and samples % (2 * LANES) == 0
        and feed_dev % 32 == 0
        and frames % 16 == 0
        and frames & (frames - 1) == 0
        and cells % 512 == 0
        and cells // parts == LANES // 2
        and trials % (2 * LANES) == 0
        and parts % 4 == 0
    )


def solution(mesh):
    parts = mesh.shape["wide"]

    def body(raw, cell_feed, dm_delay):
        if fits(parts, raw.shape, cell_feed.shape[0], dm_delay.shape):
            return tiled_body(parts, raw, cell_feed, dm_delay)
        return plain_body(raw, cell_feed, dm_delay)

    placed = (P(("grp", "wide"), None, None), P(), P())
    return jax.shard_map(
        body, mesh=mesh, in_specs=placed, out_specs=P(("grp", "wide"), None, None), check_vma=False
    )
```
